32 devices in a mesh: groups: 2 (over y), ctx: 4 (over x, core), head: 4 (over z).
Axes of the slice: x: 2, y: 2, z: 4, core: 2. Of those that a mesh axis runs over, the one named last changes fastest.
Arguments:
- context: bfloat16 [8192, 1024], P(('groups', 'ctx', 'head')), parts along dimension 0, may hold values from -6 to 6
- w_kv: bfloat16 [1024, 2048], replicated, may hold values from -0.1875 to 0.1875
- queries: bfloat16 [32, 64, 2048], P(('groups', 'head')), parts along dimension 0, may hold values from -400 to 400
- gain: float32 [1024], replicated, may hold values from 0.25 to 1.75
- w_out: bfloat16 [1024, 1024], P('head'), may hold values from -0.1875 to 0.1875
Outputs:
- latent_out: bfloat16 [4096, 1024], P(('groups', 'ctx', 'head')), parts along dimension 0
The draws below stay inside these ranges and needn't reach their ends.
There are 2 independent parts, one for each index of `groups`. The reference program is written for one: setup_inputs(seed, part) draws one part's arguments, and reference() takes and returns one part's arrays. A program takes and returns all parts, laid end to end along the dimension named above; an argument that names none is the same for every part. Nothing has to cross between parts.
All inputs are finite; a program needn't handle non-finite values.
Results may differ from the reference program's by a relative error of at most 0.01575.
Values may be sent and summed in bfloat16 or wider, within the bound.
No kernel may reach another device: no remote copies, remote signals or barrier semaphores. Data moves between devices by JAX's collectives and lax.ppermute only.
A program may use at most 64 MiB of HBM per device.

```python
import math
import jax
import jax.numpy as jnp
from jax import lax

D = 1024
H = 16
HD = 64
LAT = 2048
SEQ = 4096


def draw_queries(key, part):
    base = jnp.clip(jax.random.normal(key, (H, HD, LAT), jnp.float32), -6.0, 6.0)
    return base.astype(jnp.bfloat16)


def block_levels(stream_key, extent, cuts, low, high):
    level = 1.0
    for position, shards_of in cuts:
        steps = jax.random.uniform(jax.random.fold_in(jax.random.fold_in(stream_key, 6), position), (shards_of,), jnp.float32, low / len(cuts), high / len(cuts))
        level = level * jnp.repeat(jnp.exp(steps), extent[position] // shards_of).reshape((-1,) + (1,) * (len(extent) - 1 - position))
    return level


def normal_values(rng, extent, deviation, bound, split=(), kind=jnp.bfloat16):
    level = block_levels(rng, extent, split, -0.22, 0.18) if split else 1.0
    result = jax.random.normal(rng, extent, jnp.float32) * deviation * level
    return jnp.minimum(jnp.maximum(result, -bound), bound).astype(kind)


def setup_inputs(seed: int = 0, part: int = 0) -> dict:
    key_of = jax.random.split(jax.random.key(seed), 6)
    part_keys = jax.random.split(jax.random.fold_in(key_of[5], part), 6)
    context = normal_values(part_keys[0], (SEQ, D), 1.0, 6.0, ((0, 16),))
    w_kv = normal_values(key_of[1], (D, 2 * D), D ** -0.5, 0.1875)
    queries = draw_queries(jax.random.fold_in(jax.random.fold_in(key_of[5], part), 71), part)
    gain = jnp.clip(1.0 + 0.15 * jax.random.normal(key_of[3], (D,), jnp.float32), 0.25, 1.75)
    w_out = normal_values(key_of[4], (D, D), D ** -0.5, 0.1875, ((0, 4),))
    return {"context": context, "w_kv": w_kv, "queries": queries, "gain": gain, "w_out": w_out}


def head_attention(query_head, kv_head):
    block_size = 256
    block_count = LAT // block_size
    key_rows = kv_head[:, :HD]
    value_rows = kv_head[:, HD:]
    head_scale = 1.0 / math.sqrt(HD)
    query_blocks = query_head.reshape(HD, block_count, block_size).transpose(1, 0, 2)

    def one_block(query_block):
        scores = jnp.dot(query_block.T, key_rows.T, preferred_element_type=jnp.float32) * head_scale
        highest = lax.optimization_barrier(jnp.max(scores, axis=1, keepdims=True))
        weights = jnp.exp(scores - highest)
        row_total = lax.optimization_barrier(jnp.sum(weights, axis=1, keepdims=True))
        summed = jnp.dot(weights.astype(jnp.bfloat16), value_rows, preferred_element_type=jnp.float32)
        return summed / row_total
    outputs = lax.map(one_block, query_blocks)
    return outputs.reshape(LAT, HD)

def reference(context, w_kv, queries, gain, w_out):
    projected = jnp.dot(context, w_kv, preferred_element_type=jnp.float32).astype(jnp.bfloat16)
    kv_heads = projected.reshape(SEQ, H, 2 * HD).transpose(1, 0, 2)
    heads_out = lax.map(lambda pair: head_attention(pair[0], pair[1]), (queries, kv_heads))
    attended = heads_out.transpose(1, 0, 2).reshape(LAT, D)
    mean_square = lax.optimization_barrier(jnp.mean(attended * attended, axis=1, keepdims=True))
    normed = (attended * gain[None, :] * lax.rsqrt(mean_square + 1e-06)).astype(jnp.bfloat16)
    return jnp.dot(normed, w_out, preferred_element_type=jnp.float32).astype(jnp.bfloat16)
```

```python
import functools
import math

import jax
import jax.numpy as jnp
from jax import lax
from jax.experimental import pallas as pl
from jax.experimental.pallas import tpu as pltpu
from jax.sharding import PartitionSpec as P

epsilon = 1e-06
stat_rows = 8
f32 = jnp.float32
bf16 = jnp.bfloat16

vmem = pl.BlockSpec(memory_space=pltpu.VMEM)
anywhere = pl.BlockSpec(memory_space=pl.ANY)


def cost(flops, transcendentals, bytes_accessed):
    return pl.CostEstimate(
        flops=int(flops), transcendentals=int(transcendentals), bytes_accessed=int(bytes_accessed)
    )


def partner(value, axis, step):
    count = lax.axis_size(axis)
    return lax.ppermute(value, axis, [(i, i ^ step) for i in range(count)])


def project_kernel(chunk, chunks, width, x_ref, w_ref, *rest):
    count = (len(rest) - 2) // 1
    outs, slots, sems = rest[:count], rest[count], rest[count + 1]
    here = lax.axis_index("head")
    copies = []
    for step in range(count):
        block = (here ^ step) * chunks + chunk
        columns = pl.ds(pl.multiple_of(block * width, width), width)
        copy = pltpu.make_async_copy(w_ref.at[:, columns], slots.at[step], sems.at[step])
        copy.start()
        copies.append(copy)
    for step in list(range(1, count)) + [0]:
        copies[step].wait()
        outs[step][...] = jnp.dot(
            x_ref[...], slots[step], preferred_element_type=f32
        ).astype(bf16)


def project(context, w_kv, chunk, chunks, count):
    rows, depth = context.shape
    width = w_kv.shape[1] // (count * chunks)
    return pl.pallas_call(
        functools.partial(project_kernel, chunk, chunks, width),
        out_shape=[jax.ShapeDtypeStruct((rows, width), bf16)] * count,
        in_specs=[vmem, anywhere],
        out_specs=[vmem] * count,
        scratch_shapes=[
            pltpu.VMEM((count, depth, width), bf16),
            pltpu.SemaphoreType.DMA((count,)),
        ],
        compiler_params=pltpu.CompilerParams(vmem_limit_bytes=16 << 20),
        cost_estimate=cost(
            2 * rows * depth * width * count, 0, 2 * depth * (rows + width * count)
        ),
        name=f"project{chunk}",
    )(context, w_kv)


def split_stats(top, total):
    rows = []
    for value in (top, total):
        for _ in range(3):
            part = value.astype(bf16).astype(f32)
            rows.append(part)
            value = value - part
    pad = jnp.zeros((stat_rows - len(rows), top.shape[1]), f32)
    return jnp.concatenate(rows + [pad], axis=0).astype(bf16)


def join_stats(block):
    rows = block.astype(f32)
    return rows[0:1] + rows[1:2] + rows[2:3], rows[3:4] + rows[4:5] + rows[5:6]


def attend_kernel(count, scale, tile, q_ref, *rest):
    kv_refs, (send_ref, keep_ref, stat_ref) = rest[:count], rest[count : count + 3]
    scores_ref = rest[count + 3]
    heads, size, latents = q_ref.shape
    rows = kv_refs[0].shape[0]
    blocks = lax.axis_size("ctx")
    block = latents // blocks
    parity = lax.axis_index("ctx") & 1
    per_block = block // tile

    for head in range(heads):
        keys = [r[:, 2 * head * size : (2 * head + 1) * size] for r in kv_refs]
        values = [
            r[:, (2 * head + 1) * size : (2 * head + 2) * size].astype(f32).T.astype(bf16)
            for r in kv_refs
        ]

        def one(position, which):
            pair, part = position // per_block, position % per_block
            start = (2 * pair + which) * block + part * tile
            query = q_ref[head, :, pl.ds(pl.multiple_of(start, 128), tile)]
            top = None
            for i in range(count):
                s = jnp.dot(keys[i], query, preferred_element_type=f32)
                scores_ref[i] = s
                peak = jnp.max(s, axis=0, keepdims=True)
                top = peak if top is None else jnp.maximum(top, peak)
            total = jnp.zeros((1, tile), f32)
            summed = jnp.zeros((size, tile), f32)
            for i in range(count):
                weights = jnp.exp((scores_ref[i] - top) * scale)
                total += jnp.sum(weights, axis=0, keepdims=True)
                summed += jnp.dot(
                    values[i], weights.astype(bf16), preferred_element_type=f32
                )
            return summed, top * scale, total

        def sent(position, carry):
            summed, top, total = one(position, 1 - parity)
            lanes = pl.ds(pl.multiple_of(position * tile, 128), tile)
            send_ref[head, 0:size, lanes] = summed.astype(bf16)
            send_ref[head, size:, lanes] = split_stats(top, total)
            return carry

        def kept(position, carry):
            summed, top, total = one(position, parity)
            lanes = pl.ds(pl.multiple_of(position * tile, 128), tile)
            keep_ref[head, :, lanes] = summed
            stat_ref[head, 0:1, lanes] = top
            stat_ref[head, 1:2, lanes] = total
            return carry

        steps = (blocks // 2) * per_block
        lax.fori_loop(0, steps, sent, 0)
        lax.fori_loop(0, steps, kept, 0)


def attend(queries, parts, chunk, heads):
    count = len(parts)
    _, size, latents = queries.shape
    rows = parts[0].shape[0]
    half = latents // 2
    tile = min(256, latents // lax.axis_size("ctx"))
    work = heads * latents * rows * count
    return pl.pallas_call(
        functools.partial(attend_kernel, count, 1.0 / math.sqrt(size), tile),
        grid=(1,),
        out_shape=[
            jax.ShapeDtypeStruct((heads, size + stat_rows, half), bf16),
            jax.ShapeDtypeStruct((heads, size, half), f32),
            jax.ShapeDtypeStruct((heads, 2, half), f32),
        ],
        in_specs=[
            pl.BlockSpec((heads, size, latents), lambda i: (chunk, 0, 0)),
        ]
        + [vmem] * count,
        out_specs=[vmem] * 3,
        scratch_shapes=[pltpu.VMEM((count, rows, tile), f32)],
        compiler_params=pltpu.CompilerParams(vmem_limit_bytes=16 << 20),
        cost_estimate=cost(4 * work * size, work, 4 * heads * size * latents),
        name=f"attend{chunk}",
    )(queries, *parts)


def merge_kernel(level, last, got_ref, keep_ref, stat_ref, *outs):
    heads, size, lanes = keep_ref.shape
    block = outs[0].shape[2] if last else None
    count = lax.axis_size("ctx") >> level
    for head in range(heads):

        def merged(at):
            m_got, t_got = join_stats(got_ref[head, size:, at])
            m_own, t_own = stat_ref[head, 0:1, at], stat_ref[head, 1:2, at]
            top = jnp.maximum(m_got, m_own)
            f_got, f_own = jnp.exp(m_got - top), jnp.exp(m_own - top)
            total = t_got * f_got + t_own * f_own
            summed = got_ref[head, 0:size, at].astype(f32) * f_got + keep_ref[head, :, at] * f_own
            return summed, top, total

        if last:
            summed, _, total = merged(slice(None))
            outs[0][head] = (summed / total).astype(bf16)
            continue
        send_ref, next_ref, next_stat_ref = outs
        width = lanes // count
        parity = (lax.axis_index("ctx") >> level) & 1
        for pair in range(count // 2):
            to = slice(pair * width, (pair + 1) * width)
            at = pl.ds(pl.multiple_of((2 * pair + 1 - parity) * width, 128), width)
            summed, top, total = merged(at)
            send_ref[head, 0:size, to] = summed.astype(bf16)
            send_ref[head, size:, to] = split_stats(top, total)
            at = pl.ds(pl.multiple_of((2 * pair + parity) * width, 128), width)
            summed, top, total = merged(at)
            next_ref[head, :, to] = summed
            next_stat_ref[head, 0:1, to] = top
            next_stat_ref[head, 1:2, to] = total


def merge(level, got, keep, stat, chunk):
    heads, size, lanes = keep.shape
    last = (lax.axis_size("ctx") >> level) == 1
    if last:
        out_shape = [jax.ShapeDtypeStruct((heads, size, lanes), bf16)]
    else:
        out_shape = [
            jax.ShapeDtypeStruct((heads, size + stat_rows, lanes // 2), bf16),
            jax.ShapeDtypeStruct((heads, size, lanes // 2), f32),
            jax.ShapeDtypeStruct((heads, 2, lanes // 2), f32),
        ]
    return pl.pallas_call(
        functools.partial(merge_kernel, level, last),
        out_shape=out_shape,
        in_specs=[vmem] * 3,
        out_specs=[vmem] * len(out_shape),
        compiler_params=pltpu.CompilerParams(vmem_limit_bytes=16 << 20),
        cost_estimate=cost(4 * heads * size * lanes, 0, 10 * heads * size * lanes),
        name=f"merge{level}_{chunk}",
    )(got, keep, stat)


def gather_w_out(w_out):
    rows, columns = w_out.shape
    order = [("ctx", lax.axis_size("ctx")), ("groups", lax.axis_size("groups"))]
    pieces = math.prod(n for _, n in order)
    place = lax.axis_index("groups") * lax.axis_size("ctx") + lax.axis_index("ctx")
    piece = rows // pieces
    own = lax.dynamic_slice_in_dim(w_out, place * piece, piece, 0)
    heads = lax.axis_size("head")
    held = jnp.stack([own] + [partner(own, "head", s) for s in range(1, heads)])
    held = held.reshape(1, heads, piece, columns)
    steps = []
    bit = 2
    while bit < lax.axis_size("ctx"):
        steps.append(("ctx", bit, bit))
        bit *= 2
    bit = 1
    while bit < lax.axis_size("groups"):
        steps.append(("groups", bit, bit * lax.axis_size("ctx")))
        bit *= 2
    if lax.axis_size("ctx") > 1:
        steps.append(("ctx", 1, 1))
    offsets = [0]
    for axis, bit, weight in steps:
        held = jnp.concatenate([held, partner(held, axis, bit)], axis=0)
        offsets = offsets + [o ^ weight for o in offsets]
    inverse = [0] * pieces
    for j, o in enumerate(offsets):
        inverse[o] = j
    index = jnp.take(jnp.array(inverse, jnp.int32), jnp.arange(pieces) ^ place)
    held = jnp.take(held, index, axis=0)
    return held.transpose(1, 0, 2, 3).reshape(heads, rows, columns)


def body(context, w_kv, queries, gain, w_out):
    heads_local, size, latents = queries.shape
    width = w_kv.shape[0]
    head_count = lax.axis_size("head")
    ctx_count = lax.axis_size("ctx")
    chunks = heads_local
    heads = heads_local // chunks
    here = lax.axis_index("head")
    own_rows = latents // (ctx_count * head_count)

    w_full = gather_w_out(w_out)
    relative = here ^ jnp.arange(head_count)
    gains = jnp.take(gain.reshape(head_count, chunks, -1), relative, axis=0)

    received = []
    for chunk in range(chunks):
        parts = project(context, w_kv, chunk, chunks, head_count)
        moved = [partner(parts[s], "head", s) for s in range(head_count - 1, 0, -1)][::-1]
        received.append([parts[0]] + moved)

    blocks = []
    for chunk in range(chunks):
        send, keep, stat = attend(queries, received[chunk], chunk, heads)
        level = 0
        while (ctx_count >> level) > 1:
            got = partner(send, "ctx", 1 << level)
            level += 1
            if (ctx_count >> level) == 1:
                (done,) = merge(level, got, keep, stat, chunk)
            else:
                send, keep, stat = merge(level, got, keep, stat, chunk)
        done = done.reshape(heads * size, latents // ctx_count)
        pieces = []
        for s in range(head_count):
            piece = lax.dynamic_slice_in_dim(done, (here ^ s) * own_rows, own_rows, 1)
            pieces.append(partner(piece, "head", s) if s else piece)
        blocks.append(jnp.stack(pieces))
    joined = jnp.stack(blocks, axis=1).astype(f32)
    mean_square = jnp.sum(joined * joined, axis=(0, 1, 2)) / width
    normed = (joined * gains[..., None] * lax.rsqrt(mean_square + epsilon)).astype(bf16)
    result = lax.dot_general(
        normed.reshape(width, own_rows),
        w_full.reshape(width, -1),
        (((0,), (0,)), ((), ())),
        preferred_element_type=f32,
    )
    return result.astype(bf16)


def solution(mesh):
    return jax.shard_map(
        body,
        mesh=mesh,
        in_specs=(
            P(("groups", "ctx", "head"), None),
            P(),
            P(("groups", "head"), None, None),
            P(),
            P("head", None),
        ),
        out_specs=P(("groups", "ctx", "head"), None),
        check_vma=False,
    )
```

```python
import functools
import math

import jax
import jax.numpy as jnp
from jax import lax
from jax.experimental import pallas as pl
from jax.experimental.pallas import tpu as pltpu
from jax.sharding import PartitionSpec as P


epsilon = 1e-06
stat_rows = 8
f32 = jnp.float32
bf16 = jnp.bfloat16

vmem = pl.BlockSpec(memory_space=pltpu.VMEM)
in_hbm = pl.BlockSpec(memory_space=pltpu.HBM)


def call(kernel, out_shape, args, flops=0, transcendentals=0, scratch=(), in_specs=None):
    moved = sum(math.prod(a.shape) * a.dtype.itemsize for a in args)
    return pl.pallas_call(
        kernel,
        out_shape=out_shape,
        in_specs=in_specs or [vmem] * len(args),
        out_specs=[vmem] * len(out_shape),
        scratch_shapes=list(scratch),
        compiler_params=pltpu.CompilerParams(vmem_limit_bytes=24 << 20),
        cost_estimate=pl.CostEstimate(
            flops=int(flops), transcendentals=int(transcendentals), bytes_accessed=int(moved)
        ),
    )(*args)


def shape(dims, dtype):
    return jax.ShapeDtypeStruct(tuple(dims), dtype)


def partner(value, axis, step):
    count = lax.axis_size(axis)
    return lax.ppermute(value, axis, [(i, i ^ step) for i in range(count)])


def project_kernel(total, offset, width, size, scale, piece, x_ref, w_ref, *rest):
    count = lax.axis_size("head")
    carried_ref, rest = (rest[0], rest[1:]) if piece else (None, rest)
    outs, slots, sems = rest[:count], rest[count], rest[count + 1]
    rows = x_ref.shape[0]
    here = lax.axis_index("head")
    copies = []
    order = list(range(count - 1, -1, -1))
    for step in order:
        first = (here ^ step) * total + offset
        columns = pl.ds(pl.multiple_of(first, 128), width)
        copy = pltpu.make_async_copy(w_ref.at[:, columns], slots.at[step], sems.at[step])
        copy.start()
        copies.append(copy)
    column = lax.broadcasted_iota(jnp.int32, (1, width), 1)
    factor = jnp.where(lax.rem(column, 2 * size) < size, scale, 1.0).astype(f32)
    if piece:
        place = lax.axis_index("groups") * lax.axis_size("ctx") + lax.axis_index("ctx")
        own = carried_ref[pl.ds(pl.multiple_of(place * piece, piece), piece), :]
    for copy, step in zip(copies, order):
        copy.wait()
        product = jnp.dot(x_ref[...], slots[step], preferred_element_type=f32)
        outs[step][0:rows, :] = (product * factor).astype(bf16)
        if piece:
            for j, at in enumerate(range(0, own.shape[1], width)):
                part = own[:, at : at + width]
                outs[step][rows + j * piece : rows + (j + 1) * piece, 0 : part.shape[1]] = part


def project(context, w_kv, w_out, offset, heads, size, pieces):
    count = lax.axis_size("head")
    rows, depth = context.shape
    width = 2 * size * heads
    total = w_kv.shape[1] // count
    piece = w_out.shape[0] // pieces if w_out is not None else 0
    extra = piece * (-(-w_out.shape[1] // width)) if piece else 0
    args = [context, w_kv] + ([w_out] if piece else [])
    return call(
        functools.partial(
            project_kernel, total, 2 * size * offset, width, size, 1.0 / math.sqrt(size), piece
        ),
        [shape((rows + extra, width), bf16)] * count,
        args,
        flops=2 * rows * depth * width * count,
        scratch=[pltpu.VMEM((count, depth, width), bf16), pltpu.SemaphoreType.DMA((count,))],
        in_specs=[vmem, in_hbm] + ([vmem] if piece else []),
    )


def split_stats(top, total):
    rows = []
    for value in (top, total):
        for _ in range(3):
            part = value.astype(bf16).astype(f32)
            rows.append(part)
            value = value - part
    pad = jnp.zeros((stat_rows - len(rows), top.shape[1]), f32)
    return jnp.concatenate(rows + [pad], axis=0).astype(bf16)


def join_stats(block):
    rows = block.astype(f32)
    return rows[0:1] + rows[1:2] + rows[2:3], rows[3:4] + rows[4:5] + rows[5:6]


def attend_kernel(offset, rows, sources, tile, first, last, q_ref, *rest):
    kv_refs, rest = rest[:sources], rest[sources:]
    if not first:
        (old_ref, old_stat_ref), rest = rest[:2], rest[2:]
    outs, scores_ref = rest[:-1], rest[-1]
    _, size, latents = q_ref.shape
    heads = kv_refs[0].shape[1] // (2 * size)
    blocks = lax.axis_size("ctx")
    block = latents // blocks
    parity = lax.axis_index("ctx") & 1
    parts = block // tile
    work = [
        (head, pair, which, part)
        for head in range(heads)
        for which in range(2)
        for pair in range(blocks // 2)
        for part in range(parts)
    ]
    keys, values = {}, {}

    def lanes_of(item):
        _, pair, which, part = item
        if not last:
            return pl.ds((2 * pair + which) * block + part * tile, tile)
        which = parity if which else 1 - parity
        start = (2 * pair + which) * block + part * tile
        return pl.ds(pl.multiple_of(start, 128), tile)

    def scores(item, slot):
        head = item[0]
        if head not in keys:
            at = 2 * head * size
            keys[head] = [r[0:rows, at : at + size] for r in kv_refs]
            values[head] = [
                r[0:rows, at + size : at + 2 * size].astype(f32).T.astype(bf16) for r in kv_refs
            ]
        query = q_ref[offset + head, :, lanes_of(item)]
        top = None if first else old_stat_ref[head, 0:1, lanes_of(item)]
        for i in range(sources):
            s = jnp.dot(keys[head][i], query, preferred_element_type=f32)
            scores_ref[slot, i] = s
            peak = jnp.max(s, axis=0, keepdims=True)
            top = peak if top is None else jnp.maximum(top, peak)
        return top

    def finish(item, slot, top):
        head, pair, which, part = item
        lanes = lanes_of(item)
        if first:
            total, summed = 0.0, 0.0
        else:
            fade = jnp.exp(old_stat_ref[head, 0:1, lanes] - top)
            total = old_stat_ref[head, 1:2, lanes] * fade
            summed = old_ref[head, :, lanes] * fade
        for i in range(sources):
            weights = jnp.exp(scores_ref[slot, i] - top)
            total += jnp.sum(weights, axis=0, keepdims=True)
            summed += jnp.dot(values[head][i], weights.astype(bf16), preferred_element_type=f32)
        if not last:
            outs[0][head, :, lanes] = summed
            outs[1][head, 0:1, lanes] = top
            outs[1][head, 1:2, lanes] = total
            return
        at = pl.ds(pair * block + part * tile, tile)
        if which == 0:
            outs[0][head, 0:size, at] = summed.astype(bf16)
            outs[0][head, size:, at] = split_stats(top, total)
        else:
            outs[1][head, :, at] = summed
            outs[2][head, 0:1, at] = top
            outs[2][head, 1:2, at] = total

    top = scores(work[0], 0)
    for n, item in enumerate(work):
        later = scores(work[n + 1], (n + 1) % 2) if n + 1 < len(work) else None
        finish(item, n % 2, top)
        top = later


def attend(queries, parts, state, rows, offset, last):
    _, size, latents = queries.shape
    heads = parts[0].shape[1] // (2 * size)
    tile = min(512, latents // lax.axis_size("ctx"))
    work = heads * latents * rows * len(parts)
    half = latents // 2
    if last:
        out_shape = [
            shape((heads, size + stat_rows, half), bf16),
            shape((heads, size, half), f32),
            shape((heads, 2, half), f32),
        ]
    else:
        out_shape = [shape((heads, size, latents), f32), shape((heads, 2, latents), f32)]
    return call(
        functools.partial(attend_kernel, offset, rows, len(parts), tile, state is None, last),
        out_shape,
        [queries, *parts, *(state or ())],
        flops=4 * work * size,
        transcendentals=work,
        scratch=[pltpu.VMEM((2, len(parts), rows, tile), f32)],
    )


def merge_kernel(level, last, got_ref, keep_ref, stat_ref, *outs):
    heads, size, lanes = keep_ref.shape
    count = lax.axis_size("ctx") >> level
    others = lax.axis_size("head")
    here = lax.axis_index("head")
    for head in range(heads):

        def merged(at):
            m_got, t_got = join_stats(got_ref[head, size:, at])
            m_own, t_own = stat_ref[head, 0:1, at], stat_ref[head, 1:2, at]
            top = jnp.maximum(m_got, m_own)
            f_got, f_own = jnp.exp(m_got - top), jnp.exp(m_own - top)
            total = t_got * f_got + t_own * f_own
            summed = got_ref[head, 0:size, at].astype(f32) * f_got + keep_ref[head, :, at] * f_own
            return summed, top, total

        if last:
            own = lanes // others
            for step in range(others):
                at = pl.ds(pl.multiple_of((here ^ step) * own, 128), own)
                summed, _, total = merged(at)
                outs[step][head] = (summed / total).astype(bf16)
            continue
        send_ref, next_ref, next_stat_ref = outs
        width = lanes // count
        parity = (lax.axis_index("ctx") >> level) & 1
        for pair in range(count // 2):
            to = slice(pair * width, (pair + 1) * width)
            at = pl.ds(pl.multiple_of((2 * pair + 1 - parity) * width, 128), width)
            summed, top, total = merged(at)
            send_ref[head, 0:size, to] = summed.astype(bf16)
            send_ref[head, size:, to] = split_stats(top, total)
            at = pl.ds(pl.multiple_of((2 * pair + parity) * width, 128), width)
            summed, top, total = merged(at)
            next_ref[head, :, to] = summed
            next_stat_ref[head, 0:1, to] = top
            next_stat_ref[head, 1:2, to] = total


def merge(level, got, keep, stat):
    heads, size, lanes = keep.shape
    last = (lax.axis_size("ctx") >> level) == 1
    if last:
        others = lax.axis_size("head")
        out_shape = [shape((heads, size, lanes // others), bf16)] * others
    else:
        out_shape = [
            shape((heads, size + stat_rows, lanes // 2), bf16),
            shape((heads, size, lanes // 2), f32),
            shape((heads, 2, lanes // 2), f32),
        ]
    return call(
        functools.partial(merge_kernel, level, last),
        out_shape,
        [got, keep, stat],
        flops=4 * heads * size * lanes,
    )


def unpack_kernel(rows, piece, *refs):
    out_ref = refs[-1]
    columns = out_ref.shape[2]
    for step, ref in enumerate(refs[:-1]):
        width = ref.shape[1]
        for j, at in enumerate(range(0, columns, width)):
            wide = min(width, columns - at)
            out_ref[step, :, at : at + wide] = ref[
                rows + j * piece : rows + (j + 1) * piece, 0:wide
            ]


def pair_kernel(a_ref, b_ref, out_ref):
    out_ref[0 : a_ref.shape[0]] = a_ref[...]
    out_ref[a_ref.shape[0] :] = b_ref[...]


def order_kernel(offsets, *refs):
    out_ref = refs[-1]
    place = lax.axis_index("groups") * lax.axis_size("ctx") + lax.axis_index("ctx")
    j = 0
    for ref in refs[:-1]:
        piece = ref.shape[2]
        for i in range(ref.shape[0]):
            start = pl.multiple_of((place ^ offsets[j]) * piece, piece)
            out_ref[:, pl.ds(start, piece), :] = ref[i]
            j += 1


def gather_w_out(parts, rows, w_out, pieces):
    heads, columns = len(parts), w_out.shape[1]
    piece = w_out.shape[0] // pieces
    (held,) = call(
        functools.partial(unpack_kernel, rows, piece), [shape((heads, piece, columns), bf16)], parts
    )
    held = held.reshape(1, heads, piece, columns)
    ctx = lax.axis_size("ctx")
    steps = [("ctx", 1 << b, 1 << b) for b in range(1, (ctx - 1).bit_length())]
    steps += [
        ("groups", 1 << b, ctx << b) for b in range((lax.axis_size("groups") - 1).bit_length())
    ]
    offsets = [0]
    groups = [held]
    for n, (axis, bit, weight) in enumerate(steps):
        got = partner(held, axis, bit)
        offsets = offsets + [o ^ weight for o in offsets]
        if n + 1 < len(steps):
            (held,) = call(
                pair_kernel, [shape((2 * held.shape[0],) + held.shape[1:], bf16)], [held, got]
            )
            groups = [held]
        else:
            groups = [held, got]
    groups = groups + [partner(g, "ctx", 1) for g in groups]
    offsets = offsets + [o ^ 1 for o in offsets]
    (full,) = call(
        functools.partial(order_kernel, offsets),
        [shape((heads, w_out.shape[0], columns), bf16)],
        groups,
    )
    return full


def output_kernel(chunk_heads, x_count, *refs):
    out_ref = refs[-1]
    gain_ref, w_ref = refs[x_count], refs[x_count + 1]
    count = lax.axis_size("head")
    here = lax.axis_index("head")
    size = refs[0].shape[1]
    own = refs[0].shape[2]
    width = w_ref.shape[0] * w_ref.shape[1]
    blocks = []
    square = jnp.zeros((1, own), f32)
    for step in range(count):
        start = 0
        for n, heads in enumerate(chunk_heads):
            block = refs[n * count + step][...].reshape(heads * size, own).astype(f32)
            square += jnp.sum(block * block, axis=0, keepdims=True)
            blocks.append((step, start * size, heads * size, block))
            start += heads
    factor = lax.rsqrt(square / width + epsilon)
    factor = jnp.broadcast_to(factor, (128, own)).T[:, 0:1]
    result = jnp.zeros((own, w_ref.shape[2]), f32)
    for step, start, rows, block in blocks:
        gain = gain_ref[here ^ step, :, start : start + rows]
        normed = (block.T * gain * factor).astype(bf16)
        result += jnp.dot(
            normed, w_ref[step, start : start + rows, :], preferred_element_type=f32
        )
    out_ref[...] = result.astype(bf16)


def output(pieces, chunk_heads, gain, w_full):
    count, rows, columns = w_full.shape
    args = [p for chunk in pieces for p in chunk]
    own = args[0].shape[2]
    (result,) = call(
        functools.partial(output_kernel, chunk_heads, len(args)),
        [shape((own, columns), bf16)],
        args + [gain.reshape(count, 1, rows), w_full],
        flops=2 * own * count * rows * columns,
    )
    return result


def plain_body(context, w_kv, queries, gain, w_out):
    heads_local, head_size, latents = queries.shape
    model_width = w_kv.shape[0]
    total_heads = w_kv.shape[1] // (2 * head_size)
    head_count = lax.axis_size("head")
    ctx_count = lax.axis_size("ctx")
    head_scale = 1.0 / math.sqrt(head_size)
    projected = jnp.dot(context, w_kv, preferred_element_type=jnp.float32).astype(jnp.bfloat16)
    projected = projected.reshape(context.shape[0], total_heads, 2 * head_size)
    regrouped = lax.all_to_all(projected, "head", split_axis=1, concat_axis=0, tiled=True)
    key_rows = regrouped[:, :, :head_size]
    value_rows = regrouped[:, :, head_size:]
    block_size = min(512, latents)
    block_count = latents // block_size
    query_blocks = queries.reshape(heads_local, head_size, block_count, block_size)

    def attend(position):
        query_block = lax.dynamic_index_in_dim(query_blocks, position, 2, keepdims=False)
        scores = (
            jnp.einsum("hdq,khd->hqk", query_block, key_rows, preferred_element_type=jnp.float32)
            * head_scale
        )
        highest = jnp.max(scores, axis=2)
        weights = jnp.exp(scores - highest[:, :, None])
        row_total = jnp.sum(weights, axis=2)
        summed = jnp.einsum(
            "hqk,khd->hqd",
            weights.astype(jnp.bfloat16),
            value_rows,
            preferred_element_type=jnp.float32,
        )
        return (highest, row_total, summed)

    maxima, totals, partials = lax.map(attend, jnp.arange(block_count))
    maxima = maxima.transpose(1, 0, 2).reshape(heads_local, latents)
    totals = totals.transpose(1, 0, 2).reshape(heads_local, latents)
    partials = partials.transpose(1, 0, 2, 3).reshape(heads_local, latents * head_size // 128, 128)
    ctx_rows = latents // ctx_count
    overall = lax.pmax(maxima, "ctx")
    factor = jnp.exp(maxima - overall)
    spread = partials.reshape(heads_local, latents, head_size) * factor[:, :, None]
    scaled = spread.reshape(heads_local, latents * head_size // 128, 128)
    sums_own, total_own = (
        lax.psum_scatter(
            scaled.astype(jnp.bfloat16), "ctx", scatter_dimension=1, tiled=True
        ).astype(jnp.float32),
        lax.psum_scatter(
            (totals * factor).astype(jnp.bfloat16), "ctx", scatter_dimension=1, tiled=True
        ).astype(jnp.float32),
    )
    sums_own = sums_own.reshape(heads_local, ctx_rows, head_size)
    attended = sums_own / total_own[:, :, None]
    own_rows = ctx_rows // head_count
    packed = attended.reshape(heads_local, head_count, own_rows * head_size)
    gathered = lax.all_to_all(
        packed.astype(jnp.bfloat16), "head", split_axis=1, concat_axis=0, tiled=True
    ).astype(packed.dtype)
    joined = (
        gathered.reshape(total_heads, own_rows, head_size)
        .transpose(1, 0, 2)
        .reshape(own_rows, model_width)
    )
    mean_square = jnp.sum(joined * joined, axis=1, keepdims=True) / model_width
    normed = (joined * gain[None, :] * lax.rsqrt(mean_square + epsilon)).astype(jnp.bfloat16)
    result = jnp.dot(
        normed,
        lax.all_gather(w_out, "head", axis=0, tiled=True),
        preferred_element_type=jnp.float32,
    )
    return result.astype(jnp.bfloat16)


def fast_shapes(context, queries, w_out):
    heads_local, size, latents = queries.shape
    head_count, ctx_count = lax.axis_size("head"), lax.axis_size("ctx")
    pieces = ctx_count * lax.axis_size("groups")
    powers = (head_count, ctx_count, pieces, size)
    return (
        all(n > 0 and n & (n - 1) == 0 for n in powers)
        and (size.bit_length() - 1) % 2 == 0
        and size % 16 == 0
        and ctx_count > 1
        and head_count > 1
        and heads_local == sum(CHUNKS)
        and (latents // (ctx_count * head_count)) % 128 == 0
        and latents // ctx_count <= 512
        and context.shape[0] % 16 == 0
        and (w_out.shape[0] // pieces) % 16 == 0
    )


def body(context, w_kv, queries, gain, w_out):
    if not fast_shapes(context, queries, w_out):
        return plain_body(context, w_kv, queries, gain, w_out)
    return fast_body(context, w_kv, queries, gain, w_out)


def fast_body(context, w_kv, queries, gain, w_out):
    _, size, _ = queries.shape
    rows = context.shape[0]
    head_count = lax.axis_size("head")
    ctx_count = lax.axis_size("ctx")
    pieces = ctx_count * lax.axis_size("groups")
    chunk_heads = CHUNKS
    starts = [sum(chunk_heads[:n]) for n in range(len(chunk_heads))]

    received = []
    for n, heads in enumerate(chunk_heads):
        parts = project(context, w_kv, w_out if n == 0 else None, starts[n], heads, size, pieces)
        moved = [partner(parts[s], "head", s) for s in range(head_count - 1, 0, -1)][::-1]
        received.append([parts[0]] + moved)
    w_full = gather_w_out(received[0], rows, w_out, pieces)

    finished = []
    for n in range(len(chunk_heads)):
        state = None
        for s in range(head_count):
            state = attend(queries, [received[n][s]], state, rows, starts[n], s == head_count - 1)
        level = 0
        while (ctx_count >> level) > 1:
            got = partner(state[0], "ctx", 1 << level)
            level += 1
            state = merge(level, got, *state[1:])
        finished.append(
            [partner(state[s], "head", s) if s else state[s] for s in range(head_count)]
        )
    return output(finished, chunk_heads, gain, w_full)


CHUNKS = [2, 2]


def solution(mesh):
    return jax.shard_map(
        body,
        mesh=mesh,
        in_specs=(
            P(("groups", "ctx", "head"), None),
            P(),
            P(("groups", "head"), None, None),
            P(),
            P("head", None),
        ),
        out_specs=P(("groups", "ctx", "head"), None),
        check_vma=False,
    )
```

```python
import functools
import math

import jax
import jax.numpy as jnp
from jax import lax
from jax.experimental import pallas as pl
from jax.experimental.pallas import tpu as pltpu
from jax.sharding import PartitionSpec as P


epsilon = 1e-06
stat_rows = 8
f32 = jnp.float32
bf16 = jnp.bfloat16

vmem = pl.BlockSpec(memory_space=pltpu.VMEM)
in_hbm = pl.BlockSpec(memory_space=pltpu.HBM)


def call(kernel, out_shape, args, flops=0, transcendentals=0, scratch=(), in_specs=None):
    moved = sum(math.prod(a.shape) * a.dtype.itemsize for a in args)
    return pl.pallas_call(
        kernel,
        out_shape=out_shape,
        in_specs=in_specs or [vmem] * len(args),
        out_specs=[vmem] * len(out_shape),
        scratch_shapes=list(scratch),
        compiler_params=pltpu.CompilerParams(vmem_limit_bytes=24 << 20),
        cost_estimate=pl.CostEstimate(
            flops=int(flops), transcendentals=int(transcendentals), bytes_accessed=int(moved)
        ),
    )(*args)


def shape(dims, dtype):
    return jax.ShapeDtypeStruct(tuple(dims), dtype)


def partner(value, axis, step):
    count = lax.axis_size(axis)
    return lax.ppermute(value, axis, [(i, i ^ step) for i in range(count)])


def project_kernel(total, offset, width, size, scale, x_hbm, w_ref, *rest):
    count = lax.axis_size("head")
    outs, (x_ref, slots, x_sem, sems) = rest[:count], rest[count:]
    here = lax.axis_index("head")
    fetch = pltpu.make_async_copy(x_hbm, x_ref, x_sem)
    fetch.start()
    copies = []
    order = list(range(count - 1, -1, -1))
    for step in order:
        first = (here ^ step) * total + offset
        columns = pl.ds(pl.multiple_of(first, 128), width)
        copy = pltpu.make_async_copy(w_ref.at[:, columns], slots.at[step], sems.at[step])
        copy.start()
        copies.append(copy)
    column = lax.broadcasted_iota(jnp.int32, (1, width), 1)
    factor = jnp.where(lax.rem(column, 2 * size) < size, scale, 1.0).astype(f32)
    fetch.wait()
    for copy, step in zip(copies, order):
        copy.wait()
        product = jnp.dot(x_ref[...], slots[step], preferred_element_type=f32)
        outs[step][...] = (product * factor).astype(bf16)


def project(context, w_kv, offset, heads, size):
    count = lax.axis_size("head")
    rows, depth = context.shape
    width = 2 * size * heads
    total = w_kv.shape[1] // count
    return call(
        functools.partial(
            project_kernel, total, 2 * size * offset, width, size, 1.0 / math.sqrt(size)
        ),
        [shape((rows, width), bf16)] * count,
        [
            pltpu.with_memory_space_constraint(context, pltpu.HBM),
            pltpu.with_memory_space_constraint(w_kv, pltpu.HBM),
        ],
        flops=2 * rows * depth * width * count,
        scratch=[
            pltpu.VMEM((rows, depth), bf16),
            pltpu.VMEM((count, depth, width), bf16),
            pltpu.SemaphoreType.DMA,
            pltpu.SemaphoreType.DMA((count,)),
        ],
        in_specs=[in_hbm, in_hbm],
    )


def split_stats(top, total):
    rows = []
    for value in (top, total):
        for _ in range(3):
            part = value.astype(bf16).astype(f32)
            rows.append(part)
            value = value - part
    pad = jnp.zeros((stat_rows - len(rows), top.shape[1]), f32)
    return jnp.concatenate(rows + [pad], axis=0).astype(bf16)


def join_stats(block):
    rows = block.astype(f32)
    return rows[0:1] + rows[1:2] + rows[2:3], rows[3:4] + rows[4:5] + rows[5:6]


def attend_kernel(offset, rows, sources, tile, first, last, q_ref, *rest):
    kv_refs, rest = rest[:sources], rest[sources:]
    if not first:
        (old_ref, old_stat_ref), rest = rest[:2], rest[2:]
    outs, scores_ref = rest[:-1], rest[-1]
    _, size, latents = q_ref.shape
    heads = kv_refs[0].shape[1] // (2 * size)
    blocks = lax.axis_size("ctx")
    block = latents // blocks
    parity = lax.axis_index("ctx") & 1
    parts = block // tile
    work = [
        (head, pair, which, part)
        for head in range(heads)
        for which in range(2)
        for pair in range(blocks // 2)
        for part in range(parts)
    ]
    keys, values = {}, {}

    def lanes_of(item):
        _, pair, which, part = item
        if not last:
            return pl.ds((2 * pair + which) * block + part * tile, tile)
        which = parity if which else 1 - parity
        start = (2 * pair + which) * block + part * tile
        return pl.ds(pl.multiple_of(start, 128), tile)

    def scores(item, slot):
        head = item[0]
        if head not in keys:
            at = 2 * head * size
            keys[head] = [r[0:rows, at : at + size] for r in kv_refs]
            values[head] = [
                r[0:rows, at + size : at + 2 * size].astype(f32).T.astype(bf16) for r in kv_refs
            ]
        query = q_ref[offset + head, :, lanes_of(item)]
        top = None if first else old_stat_ref[head, 0:1, lanes_of(item)]
        for i in range(sources):
            s = jnp.dot(keys[head][i], query, preferred_element_type=f32)
            scores_ref[slot, i] = s
            peak = jnp.max(s, axis=0, keepdims=True)
            top = peak if top is None else jnp.maximum(top, peak)
        return top

    def finish(item, slot, top):
        head, pair, which, part = item
        lanes = lanes_of(item)
        if first:
            total, summed = 0.0, 0.0
        else:
            fade = jnp.exp(old_stat_ref[head, 0:1, lanes] - top)
            total = old_stat_ref[head, 1:2, lanes] * fade
            summed = old_ref[head, :, lanes] * fade
        for i in range(sources):
            weights = jnp.exp(scores_ref[slot, i] - top)
            total += jnp.sum(weights, axis=0, keepdims=True)
            summed += jnp.dot(values[head][i], weights.astype(bf16), preferred_element_type=f32)
        if not last:
            outs[0][head, :, lanes] = summed
            outs[1][head, 0:1, lanes] = top
            outs[1][head, 1:2, lanes] = total
            return
        at = pl.ds(pair * block + part * tile, tile)
        if which == 0:
            outs[0][head, 0:size, at] = summed.astype(bf16)
            outs[0][head, size:, at] = split_stats(top, total)
        else:
            outs[1][head, :, at] = summed
            outs[2][head, 0:1, at] = top
            outs[2][head, 1:2, at] = total

    top = scores(work[0], 0)
    for n, item in enumerate(work):
        later = scores(work[n + 1], (n + 1) % 2) if n + 1 < len(work) else None
        finish(item, n % 2, top)
        top = later


def attend(queries, parts, state, rows, offset, last):
    _, size, latents = queries.shape
    heads = parts[0].shape[1] // (2 * size)
    tile = min(512, latents // lax.axis_size("ctx"))
    work = heads * latents * rows * len(parts)
    half = latents // 2
    if last:
        out_shape = [
            shape((heads, size + stat_rows, half), bf16),
            shape((heads, size, half), f32),
            shape((heads, 2, half), f32),
        ]
    else:
        out_shape = [shape((heads, size, latents), f32), shape((heads, 2, latents), f32)]
    return call(
        functools.partial(attend_kernel, offset, rows, len(parts), tile, state is None, last),
        out_shape,
        [queries, *parts, *(state or ())],
        flops=4 * work * size,
        transcendentals=work,
        scratch=[pltpu.VMEM((2, len(parts), rows, tile), f32)],
    )


def merge_kernel(level, last, got_ref, keep_ref, stat_ref, *outs):
    heads, size, lanes = keep_ref.shape
    count = lax.axis_size("ctx") >> level
    others = lax.axis_size("head")
    here = lax.axis_index("head")
    for head in range(heads):

        def merged(at):
            m_got, t_got = join_stats(got_ref[head, size:, at])
            m_own, t_own = stat_ref[head, 0:1, at], stat_ref[head, 1:2, at]
            top = jnp.maximum(m_got, m_own)
            f_got, f_own = jnp.exp(m_got - top), jnp.exp(m_own - top)
            total = t_got * f_got + t_own * f_own
            summed = got_ref[head, 0:size, at].astype(f32) * f_got + keep_ref[head, :, at] * f_own
            return summed, top, total

        if last:
            own = lanes // others
            for step in range(others):
                at = pl.ds(pl.multiple_of((here ^ step) * own, 128), own)
                summed, _, total = merged(at)
                outs[step][head] = (summed / total).astype(bf16)
            continue
        send_ref, next_ref, next_stat_ref = outs
        width = lanes // count
        parity = (lax.axis_index("ctx") >> level) & 1
        for pair in range(count // 2):
            to = slice(pair * width, (pair + 1) * width)
            at = pl.ds(pl.multiple_of((2 * pair + 1 - parity) * width, 128), width)
            summed, top, total = merged(at)
            send_ref[head, 0:size, to] = summed.astype(bf16)
            send_ref[head, size:, to] = split_stats(top, total)
            at = pl.ds(pl.multiple_of((2 * pair + parity) * width, 128), width)
            summed, top, total = merged(at)
            next_ref[head, :, to] = summed
            next_stat_ref[head, 0:1, to] = top
            next_stat_ref[head, 1:2, to] = total


def merge(level, got, keep, stat):
    heads, size, lanes = keep.shape
    last = (lax.axis_size("ctx") >> level) == 1
    if last:
        others = lax.axis_size("head")
        out_shape = [shape((heads, size, lanes // others), bf16)] * others
    else:
        out_shape = [
            shape((heads, size + stat_rows, lanes // 2), bf16),
            shape((heads, size, lanes // 2), f32),
            shape((heads, 2, lanes // 2), f32),
        ]
    return call(
        functools.partial(merge_kernel, level, last),
        out_shape,
        [got, keep, stat],
        flops=4 * heads * size * lanes,
    )


def pick_kernel(piece, w_ref, out_ref, sem):
    place = lax.axis_index("groups") * lax.axis_size("ctx") + lax.axis_index("ctx")
    rows = pl.ds(pl.multiple_of(place * piece, piece), piece)
    copy = pltpu.make_async_copy(w_ref.at[rows, :], out_ref, sem)
    copy.start()
    copy.wait()


def stack_kernel(*refs):
    for n, ref in enumerate(refs[:-1]):
        refs[-1][n] = ref[...]


def order_kernel(offsets, *refs):
    out_ref = refs[-1]
    place = lax.axis_index("groups") * lax.axis_size("ctx") + lax.axis_index("ctx")
    for offset, ref in zip(offsets, refs[:-1]):
        piece = ref.shape[1]
        start = pl.multiple_of((place ^ offset) * piece, piece)
        out_ref[:, pl.ds(start, piece), :] = ref[...]


def gather_w_out(w_out, pieces):
    heads, (rows, columns) = lax.axis_size("head"), w_out.shape
    piece = rows // pieces
    (own,) = call(
        functools.partial(pick_kernel, piece),
        [shape((piece, columns), bf16)],
        [pltpu.with_memory_space_constraint(w_out, pltpu.HBM)],
        scratch=[pltpu.SemaphoreType.DMA],
        in_specs=[in_hbm],
    )
    moved = [partner(own, "head", s) for s in range(1, heads)]
    held = list(call(stack_kernel, [shape((heads, piece, columns), bf16)], [own] + moved))
    ctx = lax.axis_size("ctx")
    steps = [("ctx", 1 << b, 1 << b) for b in range(1, (ctx - 1).bit_length())]
    steps += [
        ("groups", 1 << b, ctx << b) for b in range((lax.axis_size("groups") - 1).bit_length())
    ]
    steps += [("ctx", 1, 1)]
    offsets = [0]
    for axis, bit, weight in steps:
        held = held + [partner(h, axis, bit) for h in held]
        offsets = offsets + [o ^ weight for o in offsets]
    (full,) = call(
        functools.partial(order_kernel, offsets), [shape((heads, rows, columns), bf16)], held
    )
    return full


def output_kernel(start, width, first, last, *refs):
    count = lax.axis_size("head")
    here = lax.axis_index("head")
    blocks, (gain_ref, w_ref), rest = refs[:count], refs[count : count + 2], refs[count + 2 :]
    heads, size, own = blocks[0].shape
    rows = heads * size
    square = jnp.zeros((1, own), f32) if first else rest[1][...]
    result = jnp.zeros((own, w_ref.shape[2]), f32) if first else rest[0][...]
    for step in range(count):
        block = blocks[step][...].reshape(rows, own).astype(f32)
        square += jnp.sum(block * block, axis=0, keepdims=True)
        gain = gain_ref[here ^ step, :, start : start + rows]
        result += jnp.dot(
            (block.T * gain).astype(bf16),
            w_ref[step, start : start + rows, :],
            preferred_element_type=f32,
        )
    if not last:
        rest[-2][...] = result
        rest[-1][...] = square
        return
    factor = lax.rsqrt(square / width + epsilon)
    factor = jnp.broadcast_to(factor, (128, own)).T[:, 0:1]
    rest[-1][...] = (result * factor).astype(bf16)


def output(blocks, state, start, gain, w_full, last):
    count, rows, columns = w_full.shape
    heads, size, own = blocks[0].shape
    out_shape = [shape((own, columns), bf16)] if last else [
        shape((own, columns), f32), shape((1, own), f32)
    ]
    return call(
        functools.partial(output_kernel, start * size, count * rows, state is None, last),
        out_shape,
        [*blocks, gain.reshape(count, 1, rows), w_full, *(state or ())],
        flops=2 * own * count * heads * size * columns,
    )


def plain_body(context, w_kv, queries, gain, w_out):
    heads_local, head_size, latents = queries.shape
    model_width = w_kv.shape[0]
    total_heads = w_kv.shape[1] // (2 * head_size)
    head_count = lax.axis_size("head")
    ctx_count = lax.axis_size("ctx")
    head_scale = 1.0 / math.sqrt(head_size)
    projected = jnp.dot(context, w_kv, preferred_element_type=jnp.float32).astype(jnp.bfloat16)
    projected = projected.reshape(context.shape[0], total_heads, 2 * head_size)
    regrouped = lax.all_to_all(projected, "head", split_axis=1, concat_axis=0, tiled=True)
    key_rows = regrouped[:, :, :head_size]
    value_rows = regrouped[:, :, head_size:]
    block_size = min(512, latents)
    block_count = latents // block_size
    query_blocks = queries.reshape(heads_local, head_size, block_count, block_size)

    def attend(position):
        query_block = lax.dynamic_index_in_dim(query_blocks, position, 2, keepdims=False)
        scores = (
            jnp.einsum("hdq,khd->hqk", query_block, key_rows, preferred_element_type=jnp.float32)
            * head_scale
        )
        highest = jnp.max(scores, axis=2)
        weights = jnp.exp(scores - highest[:, :, None])
        row_total = jnp.sum(weights, axis=2)
        summed = jnp.einsum(
            "hqk,khd->hqd",
            weights.astype(jnp.bfloat16),
            value_rows,
            preferred_element_type=jnp.float32,
        )
        return (highest, row_total, summed)

    maxima, totals, partials = lax.map(attend, jnp.arange(block_count))
    maxima = maxima.transpose(1, 0, 2).reshape(heads_local, latents)
    totals = totals.transpose(1, 0, 2).reshape(heads_local, latents)
    partials = partials.transpose(1, 0, 2, 3).reshape(heads_local, latents * head_size // 128, 128)
    ctx_rows = latents // ctx_count
    overall = lax.pmax(maxima, "ctx")
    factor = jnp.exp(maxima - overall)
    spread = partials.reshape(heads_local, latents, head_size) * factor[:, :, None]
    scaled = spread.reshape(heads_local, latents * head_size // 128, 128)
    sums_own, total_own = (
        lax.psum_scatter(
            scaled.astype(jnp.bfloat16), "ctx", scatter_dimension=1, tiled=True
        ).astype(jnp.float32),
        lax.psum_scatter(
            (totals * factor).astype(jnp.bfloat16), "ctx", scatter_dimension=1, tiled=True
        ).astype(jnp.float32),
    )
    sums_own = sums_own.reshape(heads_local, ctx_rows, head_size)
    attended = sums_own / total_own[:, :, None]
    own_rows = ctx_rows // head_count
    packed = attended.reshape(heads_local, head_count, own_rows * head_size)
    gathered = lax.all_to_all(
        packed.astype(jnp.bfloat16), "head", split_axis=1, concat_axis=0, tiled=True
    ).astype(packed.dtype)
    joined = (
        gathered.reshape(total_heads, own_rows, head_size)
        .transpose(1, 0, 2)
        .reshape(own_rows, model_width)
    )
    mean_square = jnp.sum(joined * joined, axis=1, keepdims=True) / model_width
    normed = (joined * gain[None, :] * lax.rsqrt(mean_square + epsilon)).astype(jnp.bfloat16)
    result = jnp.dot(
        normed,
        lax.all_gather(w_out, "head", axis=0, tiled=True),
        preferred_element_type=jnp.float32,
    )
    return result.astype(jnp.bfloat16)


def fast_shapes(context, queries, w_out):
    heads_local, size, latents = queries.shape
    head_count, ctx_count = lax.axis_size("head"), lax.axis_size("ctx")
    pieces = ctx_count * lax.axis_size("groups")
    powers = (head_count, ctx_count, pieces, size)
    return (
        all(n > 0 and n & (n - 1) == 0 for n in powers)
        and (size.bit_length() - 1) % 2 == 0
        and size % 16 == 0
        and ctx_count > 1
        and head_count > 1
        and heads_local == sum(CHUNKS)
        and (latents // (ctx_count * head_count)) % 128 == 0
        and latents // ctx_count <= 512
        and context.shape[0] % 16 == 0
        and (w_out.shape[0] // pieces) % 16 == 0
    )


def body(context, w_kv, queries, gain, w_out):
    if not fast_shapes(context, queries, w_out):
        return plain_body(context, w_kv, queries, gain, w_out)
    return fast_body(context, w_kv, queries, gain, w_out)


def fast_body(context, w_kv, queries, gain, w_out):
    _, size, _ = queries.shape
    rows = context.shape[0]
    head_count = lax.axis_size("head")
    ctx_count = lax.axis_size("ctx")
    pieces = ctx_count * lax.axis_size("groups")
    chunk_heads = CHUNKS
    starts = [sum(chunk_heads[:n]) for n in range(len(chunk_heads))]

    received = []
    for n, heads in enumerate(chunk_heads):
        parts = project(context, w_kv, starts[n], heads, size)
        moved = [partner(parts[s], "head", s) for s in range(head_count - 1, 0, -1)][::-1]
        received.append([parts[0]] + moved)
    w_full = gather_w_out(w_out, pieces)

    finished = []
    for n in range(len(chunk_heads)):
        state = None
        for s in range(head_count):
            state = attend(queries, [received[n][s]], state, rows, starts[n], s == head_count - 1)
        level = 0
        while (ctx_count >> level) > 1:
            got = partner(state[0], "ctx", 1 << level)
            level += 1
            state = merge(level, got, *state[1:])
        finished.append(
            [partner(state[s], "head", s) if s else state[s] for s in range(head_count)]
        )
    state = None
    for n in range(len(chunk_heads)):
        last = n + 1 == len(chunk_heads)
        state = output(finished[n], state, starts[n], gain, w_full, last)
    return state[0]


CHUNKS = [2, 2]


def solution(mesh):
    return jax.shard_map(
        body,
        mesh=mesh,
        in_specs=(
            P(("groups", "ctx", "head"), None),
            P(),
            P(("groups", "head"), None, None),
            P(),
            P("head", None),
        ),
        out_specs=P(("groups", "ctx", "head"), None),
        check_vma=False,
    )
```

```python
import functools
import math

import jax
import jax.numpy as jnp
from jax import lax
from jax.experimental import pallas as pl
from jax.experimental.pallas import tpu as pltpu
from jax.sharding import PartitionSpec as P


epsilon = 1e-06
stat_rows = 8
f32 = jnp.float32
bf16 = jnp.bfloat16

vmem = pl.BlockSpec(memory_space=pltpu.VMEM)
in_hbm = pl.BlockSpec(memory_space=pltpu.HBM)


def call(kernel, out_shape, args, flops=0, transcendentals=0, scratch=(), in_specs=None):
    moved = sum(math.prod(a.shape) * a.dtype.itemsize for a in args)
    return pl.pallas_call(
        kernel,
        out_shape=out_shape,
        in_specs=in_specs or [vmem] * len(args),
        out_specs=[vmem] * len(out_shape),
        scratch_shapes=list(scratch),
        compiler_params=pltpu.CompilerParams(vmem_limit_bytes=24 << 20),
        cost_estimate=pl.CostEstimate(
            flops=int(flops), transcendentals=int(transcendentals), bytes_accessed=int(moved)
        ),
    )(*args)


def shape(dims, dtype):
    return jax.ShapeDtypeStruct(tuple(dims), dtype)


def partner(value, axis, step):
    count = lax.axis_size(axis)
    return lax.ppermute(value, axis, [(i, i ^ step) for i in range(count)])


def project_kernel(plan, total, size, scale, piece, *refs):
    here = lax.axis_index("head")
    x_in, w_in, refs = refs[0], refs[1], refs[2:]
    if piece:
        o_in, refs = refs[0], refs[1:]
    outs, refs = refs[: len(plan)], refs[len(plan) :]
    copies = []
    if piece:
        (x_ref, own_ref, slots, sems, sem), at = refs, None
        place = lax.axis_index("groups") * lax.axis_size("ctx") + lax.axis_index("ctx")
        mine = pl.ds(pl.multiple_of(place * piece, piece), piece)
        fetch = pltpu.make_async_copy(x_in, x_ref, sem.at[0])
        fetch.start()
        carry = pltpu.make_async_copy(o_in.at[mine, :], own_ref, sem.at[1])
    else:
        x_ref, (slots, sems) = x_in, refs
    at = 0
    for n, (step, first, heads, _) in enumerate(plan):
        width = 2 * size * heads
        start = (here ^ step) * total + 2 * size * first
        columns = pl.ds(pl.multiple_of(start, 128), width)
        copy = pltpu.make_async_copy(
            w_in.at[:, columns], slots.at[:, at : at + width], sems.at[n]
        )
        copy.start()
        copies.append((copy, at, width))
        at += width
    if piece:
        carry.start()
        fetch.wait()
    rows = x_ref.shape[0]
    for (copy, at, width), (_, _, _, carries), out_ref in zip(copies, plan, outs):
        column = lax.broadcasted_iota(jnp.int32, (1, width), 1)
        factor = jnp.where(lax.rem(column, 2 * size) < size, scale, 1.0).astype(f32)
        copy.wait()
        product = jnp.dot(x_ref[...], slots[:, at : at + width], preferred_element_type=f32)
        out_ref[0:rows, :] = (product * factor).astype(bf16)
    if piece:
        carry.wait()
        for (_, _, width), (_, _, _, carries), out_ref in zip(copies, plan, outs):
            if carries:
                for j, at in enumerate(range(0, own_ref.shape[1], width)):
                    part = own_ref[:, at : at + width]
                    below = slice(rows + j * piece, rows + (j + 1) * piece)
                    out_ref[below, 0 : part.shape[1]] = part


def carry_kernel(x_ref, own_ref, out_ref):
    rows, width = x_ref.shape
    piece = own_ref.shape[0]
    out_ref[0:rows, :] = x_ref[...]
    for j, at in enumerate(range(0, own_ref.shape[1], width)):
        part = own_ref[:, at : at + width]
        below = slice(rows + j * piece, rows + (j + 1) * piece)
        out_ref[below, 0 : part.shape[1]] = part


def project(context, w_kv, w_out, plan, size, pieces):
    rows, depth = context.shape
    heads = sum(p[2] for p in plan)
    total = w_kv.shape[1] // lax.axis_size("head")
    piece = w_out.shape[0] // pieces if w_out is not None else 0
    out_shape = []
    for _, _, n, carries in plan:
        width = 2 * size * n
        extra = piece * (-(-w_out.shape[1] // width)) if carries else 0
        out_shape.append(shape((rows + extra, width), bf16))
    scratch = [
        pltpu.VMEM((depth, 2 * size * heads), bf16),
        pltpu.SemaphoreType.DMA((len(plan),)),
    ]
    far = functools.partial(pltpu.with_memory_space_constraint, memory_space=pltpu.HBM)
    if piece:
        args, specs = [far(context), far(w_kv), far(w_out)], [in_hbm] * 3
        out_shape += [shape(context.shape, bf16), shape((piece, w_out.shape[1]), bf16)]
        scratch.append(pltpu.SemaphoreType.DMA((2,)))
    else:
        args, specs = [context, far(w_kv)], [vmem, in_hbm]
    return call(
        functools.partial(project_kernel, plan, total, size, 1.0 / math.sqrt(size), piece),
        out_shape,
        args,
        flops=4 * rows * depth * size * heads,
        scratch=scratch,
        in_specs=specs,
    )


def split_stats(top, total):
    rows = []
    for value in (top, total):
        for _ in range(3):
            part = value.astype(bf16).astype(f32)
            rows.append(part)
            value = value - part
    pad = jnp.zeros((stat_rows - len(rows), top.shape[1]), f32)
    return jnp.concatenate(rows + [pad], axis=0).astype(bf16)


def join_stats(block):
    rows = block.astype(f32)
    return rows[0:1] + rows[1:2] + rows[2:3], rows[3:4] + rows[4:5] + rows[5:6]


def attend_kernel(offset, rows, sources, tile, first, last, q_ref, *rest):
    base = 0 if not last else offset
    kv_refs, rest = rest[:sources], rest[sources:]
    if not first:
        (old_ref, old_stat_ref), rest = rest[:2], rest[2:]
    outs, scores_ref = rest[:-1], rest[-1]
    _, size, latents = q_ref.shape
    heads = kv_refs[0].shape[1] // (2 * size)
    blocks = lax.axis_size("ctx")
    block = latents // blocks
    parity = lax.axis_index("ctx") & 1
    parts = block // tile
    work = [
        (head, pair, which, part)
        for head in range(heads)
        for which in range(2)
        for pair in range(blocks // 2)
        for part in range(parts)
    ]
    keys, values = {}, {}

    def lanes_of(item):
        _, pair, which, part = item
        if not last:
            return pl.ds((2 * pair + which) * block + part * tile, tile)
        which = parity if which else 1 - parity
        start = (2 * pair + which) * block + part * tile
        return pl.ds(pl.multiple_of(start, 128), tile)

    def scores(item, slot):
        head = item[0]
        if head not in keys:
            at = 2 * head * size
            keys[head] = [r[0:rows, at : at + size] for r in kv_refs]
            values[head] = [
                r[0:rows, at + size : at + 2 * size].astype(f32).T.astype(bf16) for r in kv_refs
            ]
        query = q_ref[offset + head, :, lanes_of(item)]
        top = None if first else old_stat_ref[base + head, 0:1, lanes_of(item)]
        for i in range(sources):
            s = jnp.dot(keys[head][i], query, preferred_element_type=f32)
            scores_ref[slot, i] = s
            peak = jnp.max(s, axis=0, keepdims=True)
            top = peak if top is None else jnp.maximum(top, peak)
        return top

    def finish(item, slot, top):
        head, pair, which, part = item
        lanes = lanes_of(item)
        if first:
            total, summed = 0.0, 0.0
        else:
            fade = jnp.exp(old_stat_ref[base + head, 0:1, lanes] - top)
            total = old_stat_ref[base + head, 1:2, lanes] * fade
            summed = old_ref[base + head, :, lanes] * fade
        for i in range(sources):
            weights = jnp.exp(scores_ref[slot, i] - top)
            total += jnp.sum(weights, axis=0, keepdims=True)
            summed += jnp.dot(values[head][i], weights.astype(bf16), preferred_element_type=f32)
        if not last:
            outs[0][head, :, lanes] = summed
            outs[1][head, 0:1, lanes] = top
            outs[1][head, 1:2, lanes] = total
            return
        at = pl.ds(pair * block + part * tile, tile)
        if which == 0:
            outs[0][head, 0:size, at] = summed.astype(bf16)
            outs[0][head, size:, at] = split_stats(top, total)
        else:
            outs[1][head, :, at] = summed
            outs[2][head, 0:1, at] = top
            outs[2][head, 1:2, at] = total

    top = scores(work[0], 0)
    for n, item in enumerate(work):
        later = scores(work[n + 1], (n + 1) % 2) if n + 1 < len(work) else None
        finish(item, n % 2, top)
        top = later


def attend(queries, parts, state, rows, offset, last):
    _, size, latents = queries.shape
    heads = parts[0].shape[1] // (2 * size)
    tile = min(512, latents // lax.axis_size("ctx"))
    work = heads * latents * rows * len(parts)
    half = latents // 2
    if last:
        out_shape = [
            shape((heads, size + stat_rows, half), bf16),
            shape((heads, size, half), f32),
            shape((heads, 2, half), f32),
        ]
    else:
        out_shape = [shape((heads, size, latents), f32), shape((heads, 2, latents), f32)]
    return call(
        functools.partial(attend_kernel, offset, rows, len(parts), tile, state is None, last),
        out_shape,
        [queries, *parts, *(state or ())],
        flops=4 * work * size,
        transcendentals=work,
        scratch=[pltpu.VMEM((2, len(parts), rows, tile), f32)],
    )


def merge_kernel(level, last, got_ref, keep_ref, stat_ref, *outs):
    heads, size, lanes = keep_ref.shape
    count = lax.axis_size("ctx") >> level
    others = lax.axis_size("head")
    here = lax.axis_index("head")
    for head in range(heads):

        def merged(at):
            m_got, t_got = join_stats(got_ref[head, size:, at])
            m_own, t_own = stat_ref[head, 0:1, at], stat_ref[head, 1:2, at]
            top = jnp.maximum(m_got, m_own)
            f_got, f_own = jnp.exp(m_got - top), jnp.exp(m_own - top)
            total = t_got * f_got + t_own * f_own
            summed = got_ref[head, 0:size, at].astype(f32) * f_got + keep_ref[head, :, at] * f_own
            return summed, top, total

        if last:
            own = lanes // others
            for step in range(others):
                at = pl.ds(pl.multiple_of((here ^ step) * own, 128), own)
                summed, _, total = merged(at)
                outs[step][head] = (summed / total).astype(bf16)
            continue
        send_ref, next_ref, next_stat_ref = outs
        width = lanes // count
        parity = (lax.axis_index("ctx") >> level) & 1
        for pair in range(count // 2):
            to = slice(pair * width, (pair + 1) * width)
            at = pl.ds(pl.multiple_of((2 * pair + 1 - parity) * width, 128), width)
            summed, top, total = merged(at)
            send_ref[head, 0:size, to] = summed.astype(bf16)
            send_ref[head, size:, to] = split_stats(top, total)
            at = pl.ds(pl.multiple_of((2 * pair + parity) * width, 128), width)
            summed, top, total = merged(at)
            next_ref[head, :, to] = summed
            next_stat_ref[head, 0:1, to] = top
            next_stat_ref[head, 1:2, to] = total


def merge(level, got, keep, stat):
    heads, size, lanes = keep.shape
    last = (lax.axis_size("ctx") >> level) == 1
    if last:
        others = lax.axis_size("head")
        out_shape = [shape((heads, size, lanes // others), bf16)] * others
    else:
        out_shape = [
            shape((heads, size + stat_rows, lanes // 2), bf16),
            shape((heads, size, lanes // 2), f32),
            shape((heads, 2, lanes // 2), f32),
        ]
    return call(
        functools.partial(merge_kernel, level, last),
        out_shape,
        [got, keep, stat],
        flops=4 * heads * size * lanes,
    )


def stack_kernel(context_rows, *refs):
    out_ref = refs[-1]
    _, piece, columns = out_ref.shape
    for step, ref in enumerate(refs[:-1]):
        rows, width = ref.shape
        if rows == piece:
            out_ref[step] = ref[...]
            continue
        for j, at in enumerate(range(0, columns, width)):
            wide = min(width, columns - at)
            here = slice(context_rows + j * piece, context_rows + (j + 1) * piece)
            out_ref[step, :, at : at + wide] = ref[here, 0:wide]


def order_kernel(offsets, *refs):
    out_ref = refs[-1]
    place = lax.axis_index("groups") * lax.axis_size("ctx") + lax.axis_index("ctx")
    for offset, ref in zip(offsets, refs[:-1]):
        piece = ref.shape[1]
        start = pl.multiple_of((place ^ offset) * piece, piece)
        out_ref[:, pl.ds(start, piece), :] = ref[...]


def gather_w_out(parts, context_rows, w_out, pieces):
    heads, (rows, columns) = len(parts), w_out.shape
    piece = rows // pieces
    held = list(
        call(
            functools.partial(stack_kernel, context_rows),
            [shape((heads, piece, columns), bf16)],
            parts,
        )
    )
    ctx = lax.axis_size("ctx")
    steps = [("ctx", 1 << b, 1 << b) for b in range(1, (ctx - 1).bit_length())]
    steps += [
        ("groups", 1 << b, ctx << b) for b in range((lax.axis_size("groups") - 1).bit_length())
    ]
    steps += [("ctx", 1, 1)]
    offsets = [0]
    for axis, bit, weight in steps:
        held = held + [partner(h, axis, bit) for h in held]
        offsets = offsets + [o ^ weight for o in offsets]
    (full,) = call(
        functools.partial(order_kernel, offsets), [shape((heads, rows, columns), bf16)], held
    )
    return full


def output_kernel(start, width, first, last, *refs):
    count = lax.axis_size("head")
    here = lax.axis_index("head")
    blocks, (gain_ref, w_ref), rest = refs[:count], refs[count : count + 2], refs[count + 2 :]
    heads, size, own = blocks[0].shape
    rows = heads * size
    square = jnp.zeros((1, own), f32) if first else rest[1][...]
    result = jnp.zeros((own, w_ref.shape[2]), f32) if first else rest[0][...]
    for step in range(count):
        block = blocks[step][...].reshape(rows, own).astype(f32)
        square += jnp.sum(block * block, axis=0, keepdims=True)
        gain = gain_ref[here ^ step, :, start : start + rows]
        result += jnp.dot(
            (block.T * gain).astype(bf16),
            w_ref[step, start : start + rows, :],
            preferred_element_type=f32,
        )
    if not last:
        rest[-2][...] = result
        rest[-1][...] = square
        return
    factor = lax.rsqrt(square / width + epsilon)
    factor = jnp.broadcast_to(factor, (128, own)).T[:, 0:1]
    rest[-1][...] = (result * factor).astype(bf16)


def output(blocks, state, start, gain, w_full, last):
    count, rows, columns = w_full.shape
    heads, size, own = blocks[0].shape
    out_shape = [shape((own, columns), bf16)] if last else [
        shape((own, columns), f32), shape((1, own), f32)
    ]
    return call(
        functools.partial(output_kernel, start * size, count * rows, state is None, last),
        out_shape,
        [*blocks, gain.reshape(count, 1, rows), w_full, *(state or ())],
        flops=2 * own * count * heads * size * columns,
    )


def plain_body(context, w_kv, queries, gain, w_out):
    heads_local, head_size, latents = queries.shape
    model_width = w_kv.shape[0]
    total_heads = w_kv.shape[1] // (2 * head_size)
    head_count = lax.axis_size("head")
    ctx_count = lax.axis_size("ctx")
    head_scale = 1.0 / math.sqrt(head_size)
    projected = jnp.dot(context, w_kv, preferred_element_type=jnp.float32).astype(jnp.bfloat16)
    projected = projected.reshape(context.shape[0], total_heads, 2 * head_size)
    regrouped = lax.all_to_all(projected, "head", split_axis=1, concat_axis=0, tiled=True)
    key_rows = regrouped[:, :, :head_size]
    value_rows = regrouped[:, :, head_size:]
    block_size = min(512, latents)
    block_count = latents // block_size
    query_blocks = queries.reshape(heads_local, head_size, block_count, block_size)

    def attend(position):
        query_block = lax.dynamic_index_in_dim(query_blocks, position, 2, keepdims=False)
        scores = (
            jnp.einsum("hdq,khd->hqk", query_block, key_rows, preferred_element_type=jnp.float32)
            * head_scale
        )
        highest = jnp.max(scores, axis=2)
        weights = jnp.exp(scores - highest[:, :, None])
        row_total = jnp.sum(weights, axis=2)
        summed = jnp.einsum(
            "hqk,khd->hqd",
            weights.astype(jnp.bfloat16),
            value_rows,
            preferred_element_type=jnp.float32,
        )
        return (highest, row_total, summed)

    maxima, totals, partials = lax.map(attend, jnp.arange(block_count))
    maxima = maxima.transpose(1, 0, 2).reshape(heads_local, latents)
    totals = totals.transpose(1, 0, 2).reshape(heads_local, latents)
    partials = partials.transpose(1, 0, 2, 3).reshape(heads_local, latents * head_size // 128, 128)
    ctx_rows = latents // ctx_count
    overall = lax.pmax(maxima, "ctx")
    factor = jnp.exp(maxima - overall)
    spread = partials.reshape(heads_local, latents, head_size) * factor[:, :, None]
    scaled = spread.reshape(heads_local, latents * head_size // 128, 128)
    sums_own, total_own = (
        lax.psum_scatter(
            scaled.astype(jnp.bfloat16), "ctx", scatter_dimension=1, tiled=True
        ).astype(jnp.float32),
        lax.psum_scatter(
            (totals * factor).astype(jnp.bfloat16), "ctx", scatter_dimension=1, tiled=True
        ).astype(jnp.float32),
    )
    sums_own = sums_own.reshape(heads_local, ctx_rows, head_size)
    attended = sums_own / total_own[:, :, None]
    own_rows = ctx_rows // head_count
    packed = attended.reshape(heads_local, head_count, own_rows * head_size)
    gathered = lax.all_to_all(
        packed.astype(jnp.bfloat16), "head", split_axis=1, concat_axis=0, tiled=True
    ).astype(packed.dtype)
    joined = (
        gathered.reshape(total_heads, own_rows, head_size)
        .transpose(1, 0, 2)
        .reshape(own_rows, model_width)
    )
    mean_square = jnp.sum(joined * joined, axis=1, keepdims=True) / model_width
    normed = (joined * gain[None, :] * lax.rsqrt(mean_square + epsilon)).astype(jnp.bfloat16)
    result = jnp.dot(
        normed,
        lax.all_gather(w_out, "head", axis=0, tiled=True),
        preferred_element_type=jnp.float32,
    )
    return result.astype(jnp.bfloat16)


def fast_shapes(context, queries, w_out):
    heads_local, size, latents = queries.shape
    head_count, ctx_count = lax.axis_size("head"), lax.axis_size("ctx")
    pieces = ctx_count * lax.axis_size("groups")
    powers = (head_count, ctx_count, pieces, size)
    return (
        all(n > 0 and n & (n - 1) == 0 for n in powers)
        and (size.bit_length() - 1) % 2 == 0
        and size % 16 == 0
        and ctx_count > 1
        and head_count > 1
        and heads_local == sum(CHUNKS)
        and (latents // (ctx_count * head_count)) % 128 == 0
        and latents // ctx_count <= 512
        and context.shape[0] % 16 == 0
        and (w_out.shape[0] // pieces) % 16 == 0
    )


def body(context, w_kv, queries, gain, w_out):
    if not fast_shapes(context, queries, w_out):
        return plain_body(context, w_kv, queries, gain, w_out)
    return fast_body(context, w_kv, queries, gain, w_out)


def fast_body(context, w_kv, queries, gain, w_out):
    heads_local, size, _ = queries.shape
    rows = context.shape[0]
    head_count = lax.axis_size("head")
    ctx_count = lax.axis_size("ctx")
    pieces = ctx_count * lax.axis_size("groups")
    starts = [sum(CHUNKS[:n]) for n in range(len(CHUNKS))]
    final = head_count // 2
    far = head_count - 1

    part, near, own = project(context, w_kv, w_out, [(far, 0, heads_local, True)], size, pieces)
    moved = {far: partner(part, "head", far)}
    others = [s for s in range(far) if s != final]
    plan = [(s, 0, heads_local, False) for s in others[::-1]]
    plan += [(final, first, n, False) for first, n in zip(starts, CHUNKS)]
    parts = project(near, w_kv, None, plan, size, pieces)
    for s, part in zip(others[::-1], parts):
        if s:
            extra = own.shape[0] * own.shape[1] // part.shape[1]
            (part,) = call(carry_kernel, [shape((rows + extra, part.shape[1]), bf16)], [part, own])
        moved[s] = partner(part, "head", s) if s else part
    late = [partner(p, "head", final) for p in parts[len(others) :]]
    riders = [
        own if s == 0 else partner(own, "head", s) if s == final else moved[s]
        for s in range(head_count)
    ]
    w_full = gather_w_out(riders, rows, w_out, pieces)
    state = None
    for s in others + [far]:
        state = attend(queries, [moved[s]], state, rows, 0, False)

    finished = []
    for n in range(len(CHUNKS)):
        sums = attend(queries, [late[n]], state, rows, starts[n], True)
        level = 0
        while (ctx_count >> level) > 1:
            got = partner(sums[0], "ctx", 1 << level)
            level += 1
            sums = merge(level, got, *sums[1:])
        finished.append([partner(sums[s], "head", s) if s else sums[s] for s in range(head_count)])
    state = None
    for n in range(len(CHUNKS)):
        last = n + 1 == len(CHUNKS)
        state = output(finished[n], state, starts[n], gain, w_full, last)
    return state[0]


CHUNKS = [2, 2]


def solution(mesh):
    return jax.shard_map(
        body,
        mesh=mesh,
        in_specs=(
            P(("groups", "ctx", "head"), None),
            P(),
            P(("groups", "head"), None, None),
            P(),
            P("head", None),
        ),
        out_specs=P(("groups", "ctx", "head"), None),
        check_vma=False,
    )
```

```python
import functools
import math

import jax
import jax.numpy as jnp
from jax import lax
from jax.experimental import pallas as pl
from jax.experimental.pallas import tpu as pltpu
from jax.sharding import PartitionSpec as P


epsilon = 1e-06
stat_rows = 8
f32 = jnp.float32
bf16 = jnp.bfloat16

vmem = pl.BlockSpec(memory_space=pltpu.VMEM)
in_hbm = pl.BlockSpec(memory_space=pltpu.HBM)


def call(kernel, out_shape, args, flops=0, transcendentals=0, scratch=(), in_specs=None):
    moved = sum(math.prod(a.shape) * a.dtype.itemsize for a in args)
    return pl.pallas_call(
        kernel,
        out_shape=out_shape,
        in_specs=in_specs or [vmem] * len(args),
        out_specs=[vmem] * len(out_shape),
        scratch_shapes=list(scratch),
        compiler_params=pltpu.CompilerParams(vmem_limit_bytes=24 << 20),
        cost_estimate=pl.CostEstimate(
            flops=int(flops), transcendentals=int(transcendentals), bytes_accessed=int(moved)
        ),
    )(*args)


def shape(dims, dtype):
    return jax.ShapeDtypeStruct(tuple(dims), dtype)


def partner(value, axis, step):
    count = lax.axis_size(axis)
    return lax.ppermute(value, axis, [(i, i ^ step) for i in range(count)])


def scaled(product, size, scale):
    column = lax.broadcasted_iota(jnp.int32, (1, product.shape[1]), 1)
    factor = jnp.where(lax.rem(column, 2 * size) < size, scale, 1.0).astype(f32)
    return (product * factor).astype(bf16)


def project_first_kernel(steps, size, scale, piece, x_hbm, w_hbm, o_hbm, *refs):
    outs, (x_ref, own_ref, slots, sems, sem) = refs[: len(steps)], refs[len(steps) :]
    width = slots.shape[2]
    here = lax.axis_index("head")
    place = lax.axis_index("groups") * lax.axis_size("ctx") + lax.axis_index("ctx")
    mine = pl.ds(pl.multiple_of(place * piece, piece), piece)
    fetch = pltpu.make_async_copy(x_hbm, x_ref, sem.at[0])
    carry = pltpu.make_async_copy(o_hbm.at[mine, :], own_ref, sem.at[1])
    fetch.start()
    copies = []
    for n, step in enumerate(steps):
        columns = pl.ds(pl.multiple_of((here ^ step) * width, 128), width)
        copies.append(pltpu.make_async_copy(w_hbm.at[:, columns], slots.at[n], sems.at[n]))
        copies[n].start()
    carry.start()
    fetch.wait()
    for n, out_ref in enumerate(outs):
        copies[n].wait()
        product = jnp.dot(x_ref[...], slots[n], preferred_element_type=f32)
        out_ref[...] = scaled(product, size, scale)
    carry.wait()


def project_first(context, w_kv, w_out, steps, size, pieces):
    rows, depth = context.shape
    width = w_kv.shape[1] // lax.axis_size("head")
    piece = w_out.shape[0] // pieces
    return call(
        functools.partial(project_first_kernel, steps, size, 1.0 / math.sqrt(size), piece),
        [shape((rows, width), bf16)] * len(steps)
        + [shape(context.shape, bf16), shape((piece, w_out.shape[1]), bf16)],
        [pltpu.with_memory_space_constraint(a, pltpu.HBM) for a in (context, w_kv, w_out)],
        flops=2 * rows * depth * width * len(steps),
        scratch=[
            pltpu.VMEM((len(steps), depth, width), bf16),
            pltpu.SemaphoreType.DMA((len(steps),)),
            pltpu.SemaphoreType.DMA((2,)),
        ],
        in_specs=[in_hbm] * 3,
    )


def project_kernel(plan, total, size, scale, x_ref, w_ref, *outs):
    here = lax.axis_index("head")
    for (step, first, heads), out_ref in zip(plan, outs):
        start = (here ^ step) * total + 2 * size * first
        columns = pl.ds(pl.multiple_of(start, 128), 2 * size * heads)
        product = jnp.dot(x_ref[...], w_ref[:, columns], preferred_element_type=f32)
        out_ref[...] = scaled(product, size, scale)


def project(context, w_kv, plan, size):
    rows, depth = context.shape
    total = w_kv.shape[1] // lax.axis_size("head")
    return call(
        functools.partial(project_kernel, plan, total, size, 1.0 / math.sqrt(size)),
        [shape((rows, 2 * size * n), bf16) for _, _, n in plan],
        [context, w_kv],
        flops=4 * rows * depth * size * sum(n for _, _, n in plan),
    )


def prepare_kernel(q_ref, out_ref):
    heads, size, _ = q_ref.shape
    for head in range(heads):
        value = q_ref[head].astype(f32) * math.log2(math.e)
        for n in range(3):
            part = value.astype(bf16)
            out_ref[head, n * size : (n + 1) * size, :] = part
            value = value - part.astype(f32)


def prepare(queries):
    heads, size, latents = queries.shape
    (out,) = call(prepare_kernel, [shape((heads, 3 * size, latents), bf16)], [queries])
    return out


def split_stats(top, total):
    rows = []
    for value in (top, total):
        for _ in range(3):
            part = value.astype(bf16).astype(f32)
            rows.append(part)
            value = value - part
    pad = jnp.zeros((stat_rows - len(rows), top.shape[1]), f32)
    return jnp.concatenate(rows + [pad], axis=0).astype(bf16)


def join_stats(block):
    rows = block.astype(f32)
    return rows[0:1] + rows[1:2] + rows[2:3], rows[3:4] + rows[4:5] + rows[5:6]


def attend_kernel(offset, rows, sources, tile, first, last, q_ref, *rest):
    base = 0 if not last else offset
    kv_refs, rest = rest[:sources], rest[sources:]
    if not first:
        (old_ref, old_stat_ref), rest = rest[:2], rest[2:]
    outs, scores_ref = rest[:-1], rest[-1]
    size, latents = q_ref.shape[1] // 3, q_ref.shape[2]
    heads = kv_refs[0].shape[1] // (2 * size)
    blocks = lax.axis_size("ctx")
    block = latents // blocks
    parity = lax.axis_index("ctx") & 1
    parts = block // tile
    work = [
        (head, pair, which, part)
        for head in range(heads)
        for which in range(2)
        for pair in range(blocks // 2)
        for part in range(parts)
    ]
    keys, values = {}, {}

    def lanes_of(item):
        _, pair, which, part = item
        if not last:
            return pl.ds((2 * pair + which) * block + part * tile, tile)
        which = parity if which else 1 - parity
        start = (2 * pair + which) * block + part * tile
        return pl.ds(pl.multiple_of(start, 128), tile)

    def scores(item, slot):
        head = item[0]
        if head not in keys:
            at = 2 * head * size
            keys[head] = [jnp.concatenate([r[0:rows, at : at + size]] * 3, axis=1) for r in kv_refs]
            values[head] = [
                jnp.concatenate(
                    [
                        r[0:rows, at + size : at + 2 * size].astype(f32).T.astype(bf16),
                        jnp.ones((16, rows), bf16),
                    ],
                    axis=0,
                )
                for r in kv_refs
            ]
        query = q_ref[offset + head, :, lanes_of(item)]
        top = None if first else old_stat_ref[base + head, 0:1, lanes_of(item)]
        for i in range(sources):
            s = jnp.dot(keys[head][i], query, preferred_element_type=f32)
            scores_ref[slot, i] = s
            peak = jnp.max(s, axis=0, keepdims=True)
            top = peak if top is None else jnp.maximum(top, peak)
        return top

    def finish(item, slot, top):
        head, pair, which, part = item
        lanes = lanes_of(item)
        if first:
            total, summed = 0.0, 0.0
        else:
            fade = jnp.exp2(old_stat_ref[base + head, 0:1, lanes] - top)
            total = old_stat_ref[base + head, 1:2, lanes] * fade
            summed = old_ref[base + head, :, lanes] * fade
        for i in range(sources):
            weights = jnp.exp2(scores_ref[slot, i] - top)
            product = jnp.dot(values[head][i], weights.astype(bf16), preferred_element_type=f32)
            total += product[size : size + 1]
            summed += product[0:size]
        if not last:
            outs[0][head, :, lanes] = summed
            outs[1][head, 0:1, lanes] = top
            outs[1][head, 1:2, lanes] = total
            return
        at = pl.ds(pair * block + part * tile, tile)
        if which == 0:
            outs[0][head, 0:size, at] = summed.astype(bf16)
            outs[0][head, size:, at] = split_stats(top, total)
        else:
            outs[1][head, :, at] = summed
            outs[2][head, 0:1, at] = top
            outs[2][head, 1:2, at] = total

    top = scores(work[0], 0)
    for n, item in enumerate(work):
        later = scores(work[n + 1], (n + 1) % 2) if n + 1 < len(work) else None
        finish(item, n % 2, top)
        top = later


def attend(queries, parts, state, rows, offset, last):
    size, latents = queries.shape[1] // 3, queries.shape[2]
    heads = parts[0].shape[1] // (2 * size)
    tile = min(512, latents // lax.axis_size("ctx"))
    work = heads * latents * rows * len(parts)
    half = latents // 2
    if last:
        out_shape = [
            shape((heads, size + stat_rows, half), bf16),
            shape((heads, size, half), f32),
            shape((heads, 2, half), f32),
        ]
    else:
        out_shape = [shape((heads, size, latents), f32), shape((heads, 2, latents), f32)]
    return call(
        functools.partial(attend_kernel, offset, rows, len(parts), tile, state is None, last),
        out_shape,
        [queries, *parts, *(state or ())],
        flops=4 * work * size,
        transcendentals=work,
        scratch=[pltpu.VMEM((2, len(parts), rows, tile), f32)],
    )


def merge_kernel(level, last, got_ref, keep_ref, stat_ref, *outs):
    heads, size, lanes = keep_ref.shape
    count = lax.axis_size("ctx") >> level
    others = lax.axis_size("head")
    here = lax.axis_index("head")
    for head in range(heads):

        def merged(at):
            m_got, t_got = join_stats(got_ref[head, size:, at])
            m_own, t_own = stat_ref[head, 0:1, at], stat_ref[head, 1:2, at]
            top = jnp.maximum(m_got, m_own)
            f_got, f_own = jnp.exp2(m_got - top), jnp.exp2(m_own - top)
            total = t_got * f_got + t_own * f_own
            summed = got_ref[head, 0:size, at].astype(f32) * f_got + keep_ref[head, :, at] * f_own
            return summed, top, total

        if last:
            own = lanes // others
            for step in range(others):
                at = pl.ds(pl.multiple_of((here ^ step) * own, 128), own)
                summed, _, total = merged(at)
                outs[step][head] = (summed / total).astype(bf16)
            continue
        send_ref, next_ref, next_stat_ref = outs
        width = lanes // count
        parity = (lax.axis_index("ctx") >> level) & 1
        for pair in range(count // 2):
            to = slice(pair * width, (pair + 1) * width)
            at = pl.ds(pl.multiple_of((2 * pair + 1 - parity) * width, 128), width)
            summed, top, total = merged(at)
            send_ref[head, 0:size, to] = summed.astype(bf16)
            send_ref[head, size:, to] = split_stats(top, total)
            at = pl.ds(pl.multiple_of((2 * pair + parity) * width, 128), width)
            summed, top, total = merged(at)
            next_ref[head, :, to] = summed
            next_stat_ref[head, 0:1, to] = top
            next_stat_ref[head, 1:2, to] = total


def merge(level, got, keep, stat):
    heads, size, lanes = keep.shape
    last = (lax.axis_size("ctx") >> level) == 1
    if last:
        others = lax.axis_size("head")
        out_shape = [shape((heads, size, lanes // others), bf16)] * others
    else:
        out_shape = [
            shape((heads, size + stat_rows, lanes // 2), bf16),
            shape((heads, size, lanes // 2), f32),
            shape((heads, 2, lanes // 2), f32),
        ]
    return call(
        functools.partial(merge_kernel, level, last),
        out_shape,
        [got, keep, stat],
        flops=4 * heads * size * lanes,
    )


def stack_kernel(*refs):
    at = 0
    for ref in refs[:-1]:
        refs[-1][at : at + ref.shape[0]] = ref[...]
        at += ref.shape[0]


def stack(blocks):
    count = sum(b.shape[0] for b in blocks)
    (whole,) = call(stack_kernel, [shape((count,) + blocks[0].shape[1:], bf16)], blocks)
    return whole


def order_kernel(offsets, index, *refs):
    out_ref = refs[-1]
    place = lax.axis_index("groups") * lax.axis_size("ctx") + lax.axis_index("ctx")
    for offset, ref in zip(offsets, refs[:-1]):
        piece = ref.shape[1]
        start = pl.multiple_of((place ^ offset) * piece, piece)
        for i, step in enumerate(index):
            out_ref[step, pl.ds(start, piece), :] = ref[i]


def gather_w_out(own, rows):
    heads, ctx = lax.axis_size("head"), lax.axis_size("ctx")
    piece, columns = own.shape
    held = own.reshape(1, piece, columns)
    index = [0]
    bit = heads // 2
    while bit:
        held = stack([held, partner(held, "head", bit)])
        index = index + [i ^ bit for i in index]
        bit //= 2
    steps = [("ctx", 1 << b, 1 << b) for b in range(1, (ctx - 1).bit_length())]
    steps += [
        ("groups", 1 << b, ctx << b) for b in range((lax.axis_size("groups") - 1).bit_length())
    ]
    steps += [("ctx", 1, 1)]
    offsets = [0]
    held = [held]
    for axis, bit, weight in steps:
        held = held + [partner(h, axis, bit) for h in held]
        offsets = offsets + [o ^ weight for o in offsets]
    (full,) = call(
        functools.partial(order_kernel, offsets, index), [shape((heads, rows, columns), bf16)], held
    )
    return full


def output_kernel(start, width, first, last, *refs):
    count = lax.axis_size("head")
    here = lax.axis_index("head")
    blocks, (gain_ref, w_ref), rest = refs[:count], refs[count : count + 2], refs[count + 2 :]
    heads, size, own = blocks[0].shape
    rows = heads * size
    square = jnp.zeros((1, own), f32) if first else rest[1][...]
    result = jnp.zeros((own, w_ref.shape[2]), f32) if first else rest[0][...]
    for step in range(count):
        block = blocks[step][...].reshape(rows, own).astype(f32)
        square += jnp.sum(block * block, axis=0, keepdims=True)
        gain = gain_ref[here ^ step, :, start : start + rows]
        result += jnp.dot(
            (block.T * gain).astype(bf16),
            w_ref[step, start : start + rows, :],
            preferred_element_type=f32,
        )
    if not last:
        rest[-2][...] = result
        rest[-1][...] = square
        return
    factor = lax.rsqrt(square / width + epsilon)
    factor = jnp.broadcast_to(factor, (128, own)).T[:, 0:1]
    rest[-1][...] = (result * factor).astype(bf16)


def output(blocks, state, start, gain, w_full, last):
    count, rows, columns = w_full.shape
    heads, size, own = blocks[0].shape
    out_shape = [shape((own, columns), bf16)] if last else [
        shape((own, columns), f32), shape((1, own), f32)
    ]
    return call(
        functools.partial(output_kernel, start * size, count * rows, state is None, last),
        out_shape,
        [*blocks, gain.reshape(count, 1, rows), w_full, *(state or ())],
        flops=2 * own * count * heads * size * columns,
    )


def plain_body(context, w_kv, queries, gain, w_out):
    heads_local, head_size, latents = queries.shape
    model_width = w_kv.shape[0]
    total_heads = w_kv.shape[1] // (2 * head_size)
    head_count = lax.axis_size("head")
    ctx_count = lax.axis_size("ctx")
    head_scale = 1.0 / math.sqrt(head_size)
    projected = jnp.dot(context, w_kv, preferred_element_type=jnp.float32).astype(jnp.bfloat16)
    projected = projected.reshape(context.shape[0], total_heads, 2 * head_size)
    regrouped = lax.all_to_all(projected, "head", split_axis=1, concat_axis=0, tiled=True)
    key_rows = regrouped[:, :, :head_size]
    value_rows = regrouped[:, :, head_size:]
    block_size = min(512, latents)
    block_count = latents // block_size
    query_blocks = queries.reshape(heads_local, head_size, block_count, block_size)

    def attend(position):
        query_block = lax.dynamic_index_in_dim(query_blocks, position, 2, keepdims=False)
        scores = (
            jnp.einsum("hdq,khd->hqk", query_block, key_rows, preferred_element_type=jnp.float32)
            * head_scale
        )
        highest = jnp.max(scores, axis=2)
        weights = jnp.exp2(scores - highest[:, :, None])
        row_total = jnp.sum(weights, axis=2)
        summed = jnp.einsum(
            "hqk,khd->hqd",
            weights.astype(jnp.bfloat16),
            value_rows,
            preferred_element_type=jnp.float32,
        )
        return (highest, row_total, summed)

    maxima, totals, partials = lax.map(attend, jnp.arange(block_count))
    maxima = maxima.transpose(1, 0, 2).reshape(heads_local, latents)
    totals = totals.transpose(1, 0, 2).reshape(heads_local, latents)
    partials = partials.transpose(1, 0, 2, 3).reshape(heads_local, latents * head_size // 128, 128)
    ctx_rows = latents // ctx_count
    overall = lax.pmax(maxima, "ctx")
    factor = jnp.exp2(maxima - overall)
    spread = partials.reshape(heads_local, latents, head_size) * factor[:, :, None]
    scaled = spread.reshape(heads_local, latents * head_size // 128, 128)
    sums_own, total_own = (
        lax.psum_scatter(
            scaled.astype(jnp.bfloat16), "ctx", scatter_dimension=1, tiled=True
        ).astype(jnp.float32),
        lax.psum_scatter(
            (totals * factor).astype(jnp.bfloat16), "ctx", scatter_dimension=1, tiled=True
        ).astype(jnp.float32),
    )
    sums_own = sums_own.reshape(heads_local, ctx_rows, head_size)
    attended = sums_own / total_own[:, :, None]
    own_rows = ctx_rows // head_count
    packed = attended.reshape(heads_local, head_count, own_rows * head_size)
    gathered = lax.all_to_all(
        packed.astype(jnp.bfloat16), "head", split_axis=1, concat_axis=0, tiled=True
    ).astype(packed.dtype)
    joined = (
        gathered.reshape(total_heads, own_rows, head_size)
        .transpose(1, 0, 2)
        .reshape(own_rows, model_width)
    )
    mean_square = jnp.sum(joined * joined, axis=1, keepdims=True) / model_width
    normed = (joined * gain[None, :] * lax.rsqrt(mean_square + epsilon)).astype(jnp.bfloat16)
    result = jnp.dot(
        normed,
        lax.all_gather(w_out, "head", axis=0, tiled=True),
        preferred_element_type=jnp.float32,
    )
    return result.astype(jnp.bfloat16)


def fast_shapes(context, queries, w_out):
    heads_local, size, latents = queries.shape
    head_count, ctx_count = lax.axis_size("head"), lax.axis_size("ctx")
    pieces = ctx_count * lax.axis_size("groups")
    powers = (head_count, ctx_count, pieces, size)
    return (
        all(n > 0 and n & (n - 1) == 0 for n in powers)
        and (size.bit_length() - 1) % 2 == 0
        and size % 16 == 0
        and ctx_count > 1
        and head_count > 2
        and heads_local == sum(CHUNKS)
        and (latents // (ctx_count * head_count)) % 128 == 0
        and latents // ctx_count <= 512
        and context.shape[0] % 16 == 0
        and (w_out.shape[0] // pieces) % 16 == 0
    )


def body(context, w_kv, queries, gain, w_out):
    if not fast_shapes(context, queries, w_out):
        return plain_body(context, w_kv, queries, gain, w_out)
    return fast_body(context, w_kv, queries, gain, w_out)


def fast_body(context, w_kv, queries, gain, w_out):
    heads_local, size, _ = queries.shape
    rows = context.shape[0]
    head_count = lax.axis_size("head")
    ctx_count = lax.axis_size("ctx")
    pieces = ctx_count * lax.axis_size("groups")
    starts = [sum(CHUNKS[:n]) for n in range(len(CHUNKS))]
    final = head_count // 2
    far = head_count - 1

    first = [s for s in range(1, head_count) if s != final]
    *sent, near, own = project_first(context, w_kv, w_out, first, size, pieces)
    w_kv, queries, near = lax.optimization_barrier((w_kv, queries, near))
    w_full = gather_w_out(own, w_out.shape[0])
    moved = {s: partner(p, "head", s) for s, p in zip(first, sent)}
    others = [s for s in range(far) if s != final]
    plan = [(0, 0, heads_local)] + [(final, f, n) for f, n in zip(starts, CHUNKS)]
    moved[0], *parts = project(near, w_kv, plan, size)
    late = [partner(p, "head", final) for p in parts]
    queries = prepare(queries)
    state = None
    for s in others + [far]:
        state = attend(queries, [moved[s]], state, rows, 0, False)

    finished = []
    for n in range(len(CHUNKS)):
        sums = attend(queries, [late[n]], state, rows, starts[n], True)
        level = 0
        while (ctx_count >> level) > 1:
            got = partner(sums[0], "ctx", 1 << level)
            level += 1
            sums = merge(level, got, *sums[1:])
        finished.append([partner(sums[s], "head", s) if s else sums[s] for s in range(head_count)])
    state = None
    for n in range(len(CHUNKS)):
        last = n + 1 == len(CHUNKS)
        state = output(finished[n], state, starts[n], gain, w_full, last)
    return state[0]


CHUNKS = [2, 2]


def solution(mesh):
    return jax.shard_map(
        body,
        mesh=mesh,
        in_specs=(
            P(("groups", "ctx", "head"), None),
            P(),
            P(("groups", "head"), None, None),
            P(),
            P("head", None),
        ),
        out_specs=P(("groups", "ctx", "head"), None),
        check_vma=False,
    )
```

```python
import functools
import math

import jax
import jax.numpy as jnp
from jax import lax
from jax.experimental import pallas as pl
from jax.experimental.pallas import tpu as pltpu
from jax.sharding import PartitionSpec as P


epsilon = 1e-06
stat_rows = 8
f32 = jnp.float32
bf16 = jnp.bfloat16

vmem = pl.BlockSpec(memory_space=pltpu.VMEM)
in_hbm = pl.BlockSpec(memory_space=pltpu.HBM)


def call(kernel, out_shape, args, flops=0, transcendentals=0, scratch=(), in_specs=None):
    moved = sum(math.prod(a.shape) * a.dtype.itemsize for a in args)
    return pl.pallas_call(
        kernel,
        out_shape=out_shape,
        in_specs=in_specs or [vmem] * len(args),
        out_specs=[vmem] * len(out_shape),
        scratch_shapes=list(scratch),
        compiler_params=pltpu.CompilerParams(vmem_limit_bytes=24 << 20),
        cost_estimate=pl.CostEstimate(
            flops=int(flops), transcendentals=int(transcendentals), bytes_accessed=int(moved)
        ),
    )(*args)


def shape(dims, dtype):
    return jax.ShapeDtypeStruct(tuple(dims), dtype)


def partner(value, axis, step):
    count = lax.axis_size(axis)
    return lax.ppermute(value, axis, [(i, i ^ step) for i in range(count)])


def scaled(product, size, scale):
    column = lax.broadcasted_iota(jnp.int32, (1, product.shape[1]), 1)
    factor = jnp.where(lax.rem(column, 2 * size) < size, scale, 1.0).astype(f32)
    return (product * factor).astype(bf16)


def project_first_kernel(steps, size, scale, piece, x_hbm, w_hbm, o_hbm, *refs):
    outs, (x_ref, own_ref, slots, sems, sem) = refs[: len(steps)], refs[len(steps) :]
    width = slots.shape[2]
    here = lax.axis_index("head")
    place = lax.axis_index("groups") * lax.axis_size("ctx") + lax.axis_index("ctx")
    mine = pl.ds(pl.multiple_of(place * piece, piece), piece)
    fetch = pltpu.make_async_copy(x_hbm, x_ref, sem.at[0])
    carry = pltpu.make_async_copy(o_hbm.at[mine, :], own_ref, sem.at[1])
    fetch.start()
    copies = []
    for n, step in enumerate(steps):
        columns = pl.ds(pl.multiple_of((here ^ step) * width, 128), width)
        copies.append(pltpu.make_async_copy(w_hbm.at[:, columns], slots.at[n], sems.at[n]))
        copies[n].start()
    carry.start()
    fetch.wait()
    for n, out_ref in enumerate(outs):
        copies[n].wait()
        product = jnp.dot(x_ref[...], slots[n], preferred_element_type=f32)
        out_ref[...] = scaled(product, size, scale)
    carry.wait()


def project_first(context, w_kv, w_out, steps, size, pieces):
    rows, depth = context.shape
    width = w_kv.shape[1] // lax.axis_size("head")
    piece = w_out.shape[0] // pieces
    return call(
        functools.partial(project_first_kernel, steps, size, 1.0 / math.sqrt(size), piece),
        [shape((rows, width), bf16)] * len(steps)
        + [shape(context.shape, bf16), shape((piece, w_out.shape[1]), bf16)],
        [pltpu.with_memory_space_constraint(a, pltpu.HBM) for a in (context, w_kv, w_out)],
        flops=2 * rows * depth * width * len(steps),
        scratch=[
            pltpu.VMEM((len(steps), depth, width), bf16),
            pltpu.SemaphoreType.DMA((len(steps),)),
            pltpu.SemaphoreType.DMA((2,)),
        ],
        in_specs=[in_hbm] * 3,
    )


def project_kernel(plan, total, size, scale, x_ref, w_ref, *outs):
    here = lax.axis_index("head")
    for (step, first, heads), out_ref in zip(plan, outs):
        start = (here ^ step) * total + 2 * size * first
        columns = pl.ds(pl.multiple_of(start, 128), 2 * size * heads)
        product = jnp.dot(x_ref[...], w_ref[:, columns], preferred_element_type=f32)
        out_ref[...] = scaled(product, size, scale)


def project(context, w_kv, plan, size):
    rows, depth = context.shape
    total = w_kv.shape[1] // lax.axis_size("head")
    return call(
        functools.partial(project_kernel, plan, total, size, 1.0 / math.sqrt(size)),
        [shape((rows, 2 * size * n), bf16) for _, _, n in plan],
        [context, w_kv],
        flops=4 * rows * depth * size * sum(n for _, _, n in plan),
    )


def prepare_kernel(q_ref, out_ref):
    heads, size, _ = q_ref.shape
    for head in range(heads):
        value = q_ref[head].astype(f32) * math.log2(math.e)
        for n in range(3):
            part = value.astype(bf16)
            out_ref[head, n * size : (n + 1) * size, :] = part
            value = value - part.astype(f32)


def prepare(queries):
    heads, size, latents = queries.shape
    (out,) = call(prepare_kernel, [shape((heads, 3 * size, latents), bf16)], [queries])
    return out


def split_stats(top, total):
    rows = []
    for value in (top, total):
        for _ in range(3):
            part = value.astype(bf16).astype(f32)
            rows.append(part)
            value = value - part
    pad = jnp.zeros((stat_rows - len(rows), top.shape[1]), f32)
    return jnp.concatenate(rows + [pad], axis=0).astype(bf16)


def join_stats(block):
    rows = block.astype(f32)
    return rows[0:1] + rows[1:2] + rows[2:3], rows[3:4] + rows[4:5] + rows[5:6]


def attend_kernel(offset, rows, sources, tile, first, last, q_ref, *rest):
    base = 0 if not last else offset
    kv_refs, rest = rest[:sources], rest[sources:]
    if not first:
        (old_ref, old_stat_ref), rest = rest[:2], rest[2:]
    outs, scores_ref = rest[:-1], rest[-1]
    size, latents = q_ref.shape[1] // 3, q_ref.shape[2]
    heads = kv_refs[0].shape[1] // (2 * size)
    blocks = lax.axis_size("ctx")
    block = latents // blocks
    parity = lax.axis_index("ctx") & 1
    parts = block // tile
    work = [
        (head, pair, which, part)
        for head in range(heads)
        for which in range(2)
        for pair in range(blocks // 2)
        for part in range(parts)
    ]
    keys, values = {}, {}

    def lanes_of(item):
        _, pair, which, part = item
        if not last:
            return pl.ds((2 * pair + which) * block + part * tile, tile)
        which = parity if which else 1 - parity
        start = (2 * pair + which) * block + part * tile
        return pl.ds(pl.multiple_of(start, 128), tile)

    def scores(item, slot):
        head = item[0]
        if head not in keys:
            at = 2 * head * size
            keys[head] = [jnp.concatenate([r[0:rows, at : at + size]] * 3, axis=1) for r in kv_refs]
            values[head] = [
                jnp.concatenate(
                    [
                        r[0:rows, at + size : at + 2 * size].astype(f32).T.astype(bf16),
                        jnp.ones((16, rows), bf16),
                    ],
                    axis=0,
                )
                for r in kv_refs
            ]
        query = q_ref[offset + head, :, lanes_of(item)]
        top = None if first else old_stat_ref[base + head, 0:1, lanes_of(item)]
        for i in range(sources):
            s = jnp.dot(keys[head][i], query, preferred_element_type=f32)
            scores_ref[slot, i] = s
            peak = jnp.max(s, axis=0, keepdims=True)
            top = peak if top is None else jnp.maximum(top, peak)
        return top

    def finish(item, slot, top):
        head, pair, which, part = item
        lanes = lanes_of(item)
        if first:
            total, summed = 0.0, 0.0
        else:
            fade = jnp.exp2(old_stat_ref[base + head, 0:1, lanes] - top)
            total = old_stat_ref[base + head, 1:2, lanes] * fade
            summed = old_ref[base + head, :, lanes] * fade
        for i in range(sources):
            weights = jnp.exp2(scores_ref[slot, i] - top)
            product = jnp.dot(values[head][i], weights.astype(bf16), preferred_element_type=f32)
            total += product[size : size + 1]
            summed += product[0:size]
        if not last:
            outs[0][head, :, lanes] = summed
            outs[1][head, 0:1, lanes] = top
            outs[1][head, 1:2, lanes] = total
            return
        at = pl.ds(pair * block + part * tile, tile)
        if which == 0:
            outs[0][head, 0:size, at] = summed.astype(bf16)
            outs[0][head, size:, at] = split_stats(top, total)
        else:
            outs[1][head, :, at] = summed
            outs[2][head, 0:1, at] = top
            outs[2][head, 1:2, at] = total

    top = scores(work[0], 0)
    for n, item in enumerate(work):
        later = scores(work[n + 1], (n + 1) % 2) if n + 1 < len(work) else None
        finish(item, n % 2, top)
        top = later


def attend(queries, parts, state, rows, offset, last):
    size, latents = queries.shape[1] // 3, queries.shape[2]
    heads = parts[0].shape[1] // (2 * size)
    tile = min(512, latents // lax.axis_size("ctx"))
    work = heads * latents * rows * len(parts)
    half = latents // 2
    if last:
        out_shape = [
            shape((heads, size + stat_rows, half), bf16),
            shape((heads, size, half), f32),
            shape((heads, 2, half), f32),
        ]
    else:
        out_shape = [shape((heads, size, latents), f32), shape((heads, 2, latents), f32)]
    return call(
        functools.partial(attend_kernel, offset, rows, len(parts), tile, state is None, last),
        out_shape,
        [queries, *parts, *(state or ())],
        flops=4 * work * size,
        transcendentals=work,
        scratch=[pltpu.VMEM((2, len(parts), rows, tile), f32)],
    )


def merge_kernel(level, last, got_ref, keep_ref, stat_ref, *outs):
    heads, size, lanes = keep_ref.shape
    count = lax.axis_size("ctx") >> level
    others = lax.axis_size("head")
    here = lax.axis_index("head")
    for head in range(heads):

        def merged(at):
            m_got, t_got = join_stats(got_ref[head, size:, at])
            m_own, t_own = stat_ref[head, 0:1, at], stat_ref[head, 1:2, at]
            top = jnp.maximum(m_got, m_own)
            f_got, f_own = jnp.exp2(m_got - top), jnp.exp2(m_own - top)
            total = t_got * f_got + t_own * f_own
            summed = got_ref[head, 0:size, at].astype(f32) * f_got + keep_ref[head, :, at] * f_own
            return summed, top, total

        if last:
            own = lanes // others
            for step in range(others):
                at = pl.ds(pl.multiple_of((here ^ step) * own, 128), own)
                summed, _, total = merged(at)
                outs[step][head] = (summed / total).astype(bf16)
            continue
        send_ref, next_ref, next_stat_ref = outs
        width = lanes // count
        parity = (lax.axis_index("ctx") >> level) & 1
        for pair in range(count // 2):
            to = slice(pair * width, (pair + 1) * width)
            at = pl.ds(pl.multiple_of((2 * pair + 1 - parity) * width, 128), width)
            summed, top, total = merged(at)
            send_ref[head, 0:size, to] = summed.astype(bf16)
            send_ref[head, size:, to] = split_stats(top, total)
            at = pl.ds(pl.multiple_of((2 * pair + parity) * width, 128), width)
            summed, top, total = merged(at)
            next_ref[head, :, to] = summed
            next_stat_ref[head, 0:1, to] = top
            next_stat_ref[head, 1:2, to] = total


def merge(level, got, keep, stat):
    heads, size, lanes = keep.shape
    last = (lax.axis_size("ctx") >> level) == 1
    if last:
        others = lax.axis_size("head")
        out_shape = [shape((heads, size, lanes // others), bf16)] * others
    else:
        out_shape = [
            shape((heads, size + stat_rows, lanes // 2), bf16),
            shape((heads, size, lanes // 2), f32),
            shape((heads, 2, lanes // 2), f32),
        ]
    return call(
        functools.partial(merge_kernel, level, last),
        out_shape,
        [got, keep, stat],
        flops=4 * heads * size * lanes,
    )


def stack_kernel(*refs):
    at = 0
    for ref in refs[:-1]:
        refs[-1][at : at + ref.shape[0]] = ref[...]
        at += ref.shape[0]


def stack(blocks):
    count = sum(b.shape[0] for b in blocks)
    (whole,) = call(stack_kernel, [shape((count,) + blocks[0].shape[1:], bf16)], blocks)
    return whole


def order_kernel(offsets, index, *refs):
    out_ref = refs[-1]
    place = lax.axis_index("groups") * lax.axis_size("ctx") + lax.axis_index("ctx")
    for offset, ref in zip(offsets, refs[:-1]):
        piece = ref.shape[1]
        start = pl.multiple_of((place ^ offset) * piece, piece)
        for i, step in enumerate(index):
            out_ref[step, pl.ds(start, piece), :] = ref[i]


def gather_w_out(own, rows):
    heads, ctx = lax.axis_size("head"), lax.axis_size("ctx")
    piece, columns = own.shape
    held = own.reshape(1, piece, columns)
    index = [0]
    bit = heads // 2
    while bit:
        held = stack([held, partner(held, "head", bit)])
        index = index + [i ^ bit for i in index]
        bit //= 2
    steps = [("ctx", 1 << b, 1 << b) for b in range(1, (ctx - 1).bit_length())]
    steps += [
        ("groups", 1 << b, ctx << b) for b in range((lax.axis_size("groups") - 1).bit_length())
    ]
    steps += [("ctx", 1, 1)]
    offsets = [0]
    held = [held]
    for axis, bit, weight in steps:
        held = held + [partner(h, axis, bit) for h in held]
        offsets = offsets + [o ^ weight for o in offsets]
    (full,) = call(
        functools.partial(order_kernel, offsets, index), [shape((heads, rows, columns), bf16)], held
    )
    return full


def output_kernel(start, width, steps, first, last, *refs):
    count = len(steps)
    here = lax.axis_index("head")
    blocks, (gain_ref, w_ref), rest = refs[:count], refs[count : count + 2], refs[count + 2 :]
    heads, size, own = blocks[0].shape
    rows = heads * size
    square = jnp.zeros((1, own), f32) if first else rest[1][...]
    result = jnp.zeros((own, w_ref.shape[2]), f32) if first else rest[0][...]
    for step, block_ref in zip(steps, blocks):
        block = block_ref[...].reshape(rows, own).astype(f32)
        square += jnp.sum(block * block, axis=0, keepdims=True)
        gain = gain_ref[here ^ step, :, start : start + rows]
        result += jnp.dot(
            (block.T * gain).astype(bf16),
            w_ref[step, start : start + rows, :],
            preferred_element_type=f32,
        )
    if not last:
        rest[-2][...] = result
        rest[-1][...] = square
        return
    factor = lax.rsqrt(square / width + epsilon)
    factor = jnp.broadcast_to(factor, (128, own)).T[:, 0:1]
    rest[-1][...] = (result * factor).astype(bf16)


def output(blocks, steps, state, start, gain, w_full, last):
    count, rows, columns = w_full.shape
    heads, size, own = blocks[0].shape
    out_shape = [shape((own, columns), bf16)] if last else [
        shape((own, columns), f32), shape((1, own), f32)
    ]
    return call(
        functools.partial(output_kernel, start * size, count * rows, steps, state is None, last),
        out_shape,
        [*blocks, gain.reshape(count, 1, rows), w_full, *(state or ())],
        flops=2 * own * count * heads * size * columns,
    )


def plain_body(context, w_kv, queries, gain, w_out):
    heads_local, head_size, latents = queries.shape
    model_width = w_kv.shape[0]
    total_heads = w_kv.shape[1] // (2 * head_size)
    head_count = lax.axis_size("head")
    ctx_count = lax.axis_size("ctx")
    head_scale = 1.0 / math.sqrt(head_size)
    projected = jnp.dot(context, w_kv, preferred_element_type=jnp.float32).astype(jnp.bfloat16)
    projected = projected.reshape(context.shape[0], total_heads, 2 * head_size)
    regrouped = lax.all_to_all(projected, "head", split_axis=1, concat_axis=0, tiled=True)
    key_rows = regrouped[:, :, :head_size]
    value_rows = regrouped[:, :, head_size:]
    block_size = min(512, latents)
    block_count = latents // block_size
    query_blocks = queries.reshape(heads_local, head_size, block_count, block_size)

    def attend(position):
        query_block = lax.dynamic_index_in_dim(query_blocks, position, 2, keepdims=False)
        scores = (
            jnp.einsum("hdq,khd->hqk", query_block, key_rows, preferred_element_type=jnp.float32)
            * head_scale
        )
        highest = jnp.max(scores, axis=2)
        weights = jnp.exp2(scores - highest[:, :, None])
        row_total = jnp.sum(weights, axis=2)
        summed = jnp.einsum(
            "hqk,khd->hqd",
            weights.astype(jnp.bfloat16),
            value_rows,
            preferred_element_type=jnp.float32,
        )
        return (highest, row_total, summed)

    maxima, totals, partials = lax.map(attend, jnp.arange(block_count))
    maxima = maxima.transpose(1, 0, 2).reshape(heads_local, latents)
    totals = totals.transpose(1, 0, 2).reshape(heads_local, latents)
    partials = partials.transpose(1, 0, 2, 3).reshape(heads_local, latents * head_size // 128, 128)
    ctx_rows = latents // ctx_count
    overall = lax.pmax(maxima, "ctx")
    factor = jnp.exp2(maxima - overall)
    spread = partials.reshape(heads_local, latents, head_size) * factor[:, :, None]
    scaled = spread.reshape(heads_local, latents * head_size // 128, 128)
    sums_own, total_own = (
        lax.psum_scatter(
            scaled.astype(jnp.bfloat16), "ctx", scatter_dimension=1, tiled=True
        ).astype(jnp.float32),
        lax.psum_scatter(
            (totals * factor).astype(jnp.bfloat16), "ctx", scatter_dimension=1, tiled=True
        ).astype(jnp.float32),
    )
    sums_own = sums_own.reshape(heads_local, ctx_rows, head_size)
    attended = sums_own / total_own[:, :, None]
    own_rows = ctx_rows // head_count
    packed = attended.reshape(heads_local, head_count, own_rows * head_size)
    gathered = lax.all_to_all(
        packed.astype(jnp.bfloat16), "head", split_axis=1, concat_axis=0, tiled=True
    ).astype(packed.dtype)
    joined = (
        gathered.reshape(total_heads, own_rows, head_size)
        .transpose(1, 0, 2)
        .reshape(own_rows, model_width)
    )
    mean_square = jnp.sum(joined * joined, axis=1, keepdims=True) / model_width
    normed = (joined * gain[None, :] * lax.rsqrt(mean_square + epsilon)).astype(jnp.bfloat16)
    result = jnp.dot(
        normed,
        lax.all_gather(w_out, "head", axis=0, tiled=True),
        preferred_element_type=jnp.float32,
    )
    return result.astype(jnp.bfloat16)


def fast_shapes(context, queries, w_out):
    heads_local, size, latents = queries.shape
    head_count, ctx_count = lax.axis_size("head"), lax.axis_size("ctx")
    pieces = ctx_count * lax.axis_size("groups")
    powers = (head_count, ctx_count, pieces, size)
    return (
        all(n > 0 and n & (n - 1) == 0 for n in powers)
        and (size.bit_length() - 1) % 2 == 0
        and size % 16 == 0
        and ctx_count > 1
        and head_count > 2
        and heads_local == sum(CHUNKS)
        and (latents // (ctx_count * head_count)) % 128 == 0
        and latents // ctx_count <= 512
        and context.shape[0] % 16 == 0
        and (w_out.shape[0] // pieces) % 16 == 0
    )


def body(context, w_kv, queries, gain, w_out):
    if not fast_shapes(context, queries, w_out):
        return plain_body(context, w_kv, queries, gain, w_out)
    return fast_body(context, w_kv, queries, gain, w_out)


def fast_body(context, w_kv, queries, gain, w_out):
    heads_local, size, _ = queries.shape
    rows = context.shape[0]
    head_count = lax.axis_size("head")
    ctx_count = lax.axis_size("ctx")
    pieces = ctx_count * lax.axis_size("groups")
    starts = [sum(CHUNKS[:n]) for n in range(len(CHUNKS))]
    final = head_count // 2
    far = head_count - 1

    first = [s for s in range(1, head_count) if s != final]
    *sent, near, own = project_first(context, w_kv, w_out, first, size, pieces)
    w_kv, queries, near = lax.optimization_barrier((w_kv, queries, near))
    w_full = gather_w_out(own, w_out.shape[0])
    moved = {s: partner(p, "head", s) for s, p in zip(first, sent)}
    others = [s for s in range(far) if s != final]
    plan = [(0, 0, heads_local)] + [(final, f, n) for f, n in zip(starts, CHUNKS)]
    moved[0], *parts = project(near, w_kv, plan, size)
    late = [partner(p, "head", final) for p in parts]
    queries = prepare(queries)
    state = None
    for s in others + [far]:
        state = attend(queries, [moved[s]], state, rows, 0, False)

    finished = []
    for n in range(len(CHUNKS)):
        sums = attend(queries, [late[n]], state, rows, starts[n], True)
        level = 0
        while (ctx_count >> level) > 1:
            got = partner(sums[0], "ctx", 1 << level)
            level += 1
            sums = merge(level, got, *sums[1:])
        finished.append([partner(sums[s], "head", s) if s else sums[s] for s in range(head_count)])
    jobs = [(n, tuple(range(head_count))) for n in range(len(CHUNKS))]
    n, steps = jobs.pop()
    jobs += [(n, steps[:1] + steps[2:]), (n, steps[1:2])]
    state = None
    for i, (n, steps) in enumerate(jobs):
        blocks = [finished[n][s] for s in steps]
        last = i + 1 == len(jobs)
        state = output(blocks, steps, state, starts[n], gain, w_full, last)
    return state[0]


CHUNKS = [2, 2]


def solution(mesh):
    return jax.shard_map(
        body,
        mesh=mesh,
        in_specs=(
            P(("groups", "ctx", "head"), None),
            P(),
            P(("groups", "head"), None, None),
            P(),
            P("head", None),
        ),
        out_specs=P(("groups", "ctx", "head"), None),
        check_vma=False,
    )
```
